128 devices in a mesh: neg: 16 (over y, z), rep: 8 (over x, core).
Axes of the slice: x: 4, y: 4, z: 4, core: 2. Of those that a mesh axis runs over, the one named last changes fastest.
Arguments:
- goal_states: bfloat16 [8, 128, 128, 512], P('rep', 'neg'), may hold values from -6 to 6
- premise_states: bfloat16 [8, 512, 128, 512], P('rep', 'neg'), may hold values from -6 to 6
- goal_ids: int32 [8, 128, 128], P('rep', 'neg'), may hold values from 0 to 31999, as said below
- premise_ids: int32 [8, 512, 128], P('rep', 'neg'), may hold values from 0 to 31999, as said below
- positives: int32 [8, 128], P('rep'), may hold values from 0 to 511
- depthwise_kernels: float32 [2, 3, 512], replicated, may hold values from -3.5 to 3.5
- block_norm_gains: float32 [2, 512], replicated, may hold values from 0.25 to 1.75
- pointwise_weights: bfloat16 [2, 512, 512], replicated, may hold values from -0.25 to 0.25
- head_weight: bfloat16 [512, 256], replicated, may hold values from -0.25 to 0.25
Outputs:
- goal_loss: float32 [8, 128], P('rep', 'neg')
- grad_depth: float32 [2, 3, 512], replicated
- grad_gain: float32 [2, 512], replicated
- grad_point: float32 [2, 512, 512], replicated
- grad_head: float32 [512, 256], replicated
The draws below stay inside these ranges and needn't reach their ends.
Inputs may be any that keep to these rules, and one draw needn't show every extreme that they name: `goal_ids`: id 0 marks padding: a sequence's ids are nonzero on its first positions and 0 after them, with at least 16 nonzero ids. `premise_ids`: id 0 marks padding: a sequence's ids are nonzero on its first positions and 0 after them, with at least 16 nonzero ids.
All inputs are finite; a program needn't handle non-finite values.
Results may differ from the reference program's by a relative error of at most 0.022.
Values may be sent and summed in bfloat16 or wider, within the bound.
No kernel may reach another device: no remote copies, remote signals or barrier semaphores. Data moves between devices by JAX's collectives and lax.ppermute only.
A program may use at most 192 MiB of HBM per device.

```python
import jax
import jax.numpy as jnp
from jax import lax

D = 512
E = 256
L = 128
K = 3
LOWER_DILATION = 4
UPPER_DILATION = 8
VOCAB = 32000
G_DEV = 8
P_DEV = 32
GOALS_GRP = 128
PREM_GRP = 512
N_NEG = 16
N_REP = 8


def padded_ids(key, leading):
    key_length, key_token = jax.random.split(key)
    lengths = jax.random.randint(key_length, leading, L // 8, L + 1)
    tokens = jax.random.randint(key_token, leading + (L,), 1, VOCAB)
    places = jnp.arange(L)
    return jnp.where(places < lengths[..., None], tokens, 0).astype(jnp.int32)


def draw_goal_ids(key, part):
    return padded_ids(jax.random.fold_in(key, 11), (N_REP, GOALS_GRP))


def draw_premise_ids(key, part):
    return padded_ids(jax.random.fold_in(key, 23), (N_REP, PREM_GRP))


def set_ends(result, key, smallest, high):
    longest = result.shape.index(max(result.shape))
    spots = []
    for shift in (0, 1):
        where = [jax.random.randint(jax.random.fold_in(key, axis), (), 0, length) for axis, length in enumerate(result.shape)]
        where[longest] = (where[longest] + shift) % result.shape[longest]
        spots.append(tuple(where))
    return result.at[spots[0]].set(smallest).at[spots[1]].set(high)


def with_spikes(entries, stream_key, source, target, shards_of, factor):
    def block_of(position):
        return (jnp.arange(entries.shape[position]) // (entries.shape[position] // shards_of)).reshape((-1,) + (1,) * (entries.ndim - 1 - position))

    near = jax.random.permutation(stream_key, shards_of)[block_of(target)]
    other_side = (block_of(target) + shards_of // 2) % shards_of
    return jnp.where((block_of(source) == near) | (block_of(source) == other_side), factor * entries, entries)


def steps_of(key, dims, pieces, low, largest):
    factor_of, own = 1.0, jax.random.fold_in(key, 6)
    for dim, shards_of in pieces:
        draws = jnp.exp(jax.random.uniform(jax.random.fold_in(own, dim), (shards_of,), jnp.float32, low / len(pieces), largest / len(pieces)))
        factor_of = factor_of * jnp.repeat(draws, dims[dim] // shards_of).reshape([-1 if axis == dim else 1 for axis in range(len(dims))])
    return factor_of


def gaussian(key, extent, spread, limit, cuts=(), kind=jnp.bfloat16):
    drawn = jax.random.normal(key, extent, jnp.float32) * spread
    if len(cuts) > 0:
        drawn = steps_of(key, extent, cuts, -0.22, 0.18) * drawn
    return jnp.clip(drawn, min=-limit, max=limit).astype(kind)


def noise_with(rng, extent, deviation, bound, pieces, heavy, kind=jnp.bfloat16):
    drawn = deviation * jax.random.normal(rng, extent, jnp.float32)
    if pieces:
        drawn = drawn * steps_of(rng, extent, pieces, -0.22, 0.18)
    return jnp.clip(with_spikes(drawn, jax.random.fold_in(rng, 3), *heavy), -bound, bound).astype(kind)


def setup_inputs(seed: int = 0) -> dict:
    key_of = jax.random.split(jax.random.key(seed), 10)
    return {
        "goal_states": noise_with(key_of[0], (N_REP, GOALS_GRP, L, D), 1.0, 6.0, ((0, 8), (1, 16)), (1, 3, 16, 2.0)),
        "premise_states": noise_with(key_of[1], (N_REP, PREM_GRP, L, D), 1.0, 6.0, ((0, 8), (1, 16)), (1, 3, 16, 2.0)),
        "goal_ids": draw_goal_ids(jax.random.fold_in(key_of[9], 71), 0),
        "premise_ids": draw_premise_ids(jax.random.fold_in(key_of[9], 71), 0),
        "positives": set_ends(jax.random.randint(key_of[4], (N_REP, GOALS_GRP), 0, PREM_GRP), jax.random.fold_in(key_of[4], 1), 0, PREM_GRP - 1).astype(jnp.int32),
        "depthwise_kernels": gaussian(key_of[5], (2, K, D), K ** -0.5, 3.5, (), jnp.float32),
        "block_norm_gains": jnp.clip(1.0 + 0.15 * jax.random.normal(key_of[6], (2, D), jnp.float32), 0.25, 1.75),
        "pointwise_weights": gaussian(key_of[7], (2, D, D), D ** -0.5, 0.25),
        "head_weight": gaussian(key_of[8], (D, E), D ** -0.5, 0.25),
    }


logit_scale = 20.0

def shift_down(values, dilation):
    return jnp.pad(values, ((0, 0), (dilation, 0), (0, 0)))[:, :values.shape[1]]

def shift_up(values, dilation):
    return jnp.pad(values, ((0, 0), (0, dilation), (0, 0)))[:, dilation:]

def depth_conv(inputs, kernel, dilation):
    return kernel[0] * shift_down(inputs, dilation) + kernel[1] * inputs + kernel[2] * shift_up(inputs, dilation)

def conv_block_forward(hidden, kernel, gain, weight, token_valid_mask, dilation):
    widened = hidden.astype(jnp.float32)
    inverse = lax.rsqrt(lax.optimization_barrier(jnp.mean(widened * widened, axis=-1, keepdims=True)) + 1e-06)
    normed = widened * inverse * gain * token_valid_mask
    mixed = depth_conv(normed, kernel, dilation).astype(jnp.bfloat16)
    count, length, width = hidden.shape
    pre_act = jnp.dot(mixed.reshape(count * length, width), weight, preferred_element_type=jnp.float32).reshape(count, length, width)
    output = (widened + jax.nn.gelu(pre_act, approximate=True)).astype(jnp.bfloat16)
    return (output, (inverse, mixed, pre_act))

def conv_block_backward(upstream, hidden, saved, kernel, gain, weight, token_valid_mask, dilation, need_input):
    inverse, mixed, pre_act = saved
    widened = hidden.astype(jnp.float32)
    normed = widened * inverse * gain * token_valid_mask
    ignored_value, gelu_back = jax.vjp(lambda value: jax.nn.gelu(value, approximate=True), pre_act)
    act_grad = gelu_back(upstream)[0].astype(jnp.bfloat16)
    count, length, width = hidden.shape
    flat_grad = act_grad.reshape(count * length, width)
    grad_weight = jnp.dot(mixed.reshape(count * length, width).T, flat_grad, preferred_element_type=jnp.float32)
    conv_grad = jnp.dot(flat_grad, weight.T, preferred_element_type=jnp.float32).reshape(count, length, width)
    grad_kernel = jnp.stack([lax.optimization_barrier(jnp.sum(shift_down(normed, dilation) * conv_grad, axis=(0, 1))), lax.optimization_barrier(jnp.sum(normed * conv_grad, axis=(0, 1))), lax.optimization_barrier(jnp.sum(shift_up(normed, dilation) * conv_grad, axis=(0, 1)))])
    normed_grad = (kernel[0] * shift_up(conv_grad, dilation) + kernel[1] * conv_grad + kernel[2] * shift_down(conv_grad, dilation)) * token_valid_mask
    grad_gain = lax.optimization_barrier(jnp.sum(normed_grad * widened * inverse, axis=(0, 1)))
    input_grad = None
    if need_input:
        scaled = normed_grad * gain
        input_grad = upstream + inverse * scaled - widened * inverse ** 3 * lax.optimization_barrier(jnp.mean(scaled * widened, axis=-1, keepdims=True))
    return (input_grad, grad_kernel, grad_gain, grad_weight)

def pool_forward(hidden, token_valid_mask, head_weight):
    widened = hidden.astype(jnp.float32)
    counts = lax.optimization_barrier(jnp.sum(token_valid_mask, axis=1))
    pooled = (lax.optimization_barrier(jnp.sum(widened * token_valid_mask, axis=1)) / counts).astype(jnp.bfloat16)
    embedded = jnp.dot(pooled, head_weight, preferred_element_type=jnp.float32)
    magnitude = jnp.sqrt(lax.optimization_barrier(jnp.sum(embedded * embedded, axis=-1, keepdims=True)) + 1e-06)
    unit = embedded / magnitude
    return (unit.astype(jnp.bfloat16), (counts, pooled, unit, magnitude))

def pool_backward(unit_grad, saved, token_valid_mask, head_weight):
    counts, pooled, unit, magnitude = saved
    embed_grad = ((unit_grad - unit * lax.optimization_barrier(jnp.sum(unit * unit_grad, axis=-1, keepdims=True))) / magnitude).astype(jnp.bfloat16)
    grad_head = jnp.dot(pooled.T, embed_grad, preferred_element_type=jnp.float32)
    pooled_grad = jnp.dot(embed_grad, head_weight.T, preferred_element_type=jnp.float32)
    hidden_gradient = (pooled_grad / counts)[:, None, :] * token_valid_mask
    return (hidden_gradient, grad_head)

def encode(token_states, token_ids, depthwise_kernels, block_norm_gains, pointwise_weights, head_weight):
    token_valid_mask = (token_ids != 0).astype(jnp.float32)[..., None]
    first_hidden, lower_residuals = conv_block_forward(token_states, depthwise_kernels[0], block_norm_gains[0], pointwise_weights[0], token_valid_mask, LOWER_DILATION)
    second_hidden, upper_residuals = conv_block_forward(first_hidden, depthwise_kernels[1], block_norm_gains[1], pointwise_weights[1], token_valid_mask, UPPER_DILATION)
    unit_half, saved_pool = pool_forward(second_hidden, token_valid_mask, head_weight)
    return (unit_half, (token_valid_mask, first_hidden, lower_residuals, upper_residuals, saved_pool))

def device_grads(token_states, token_ids, unit_grad, depthwise_kernels, block_norm_gains, pointwise_weights, head_weight):
    unit_half, saved = encode(token_states, token_ids, depthwise_kernels, block_norm_gains, pointwise_weights, head_weight)
    token_valid_mask, first_hidden, lower_residuals, upper_residuals, saved_pool = saved
    hidden_gradient, grad_head = pool_backward(unit_grad, saved_pool, token_valid_mask, head_weight)
    lower_gradient, upper_kernel, upper_gain, upper_weight = conv_block_backward(hidden_gradient, first_hidden, upper_residuals, depthwise_kernels[1], block_norm_gains[1], pointwise_weights[1], token_valid_mask, UPPER_DILATION, True)
    ignored_value, lower_kernel, lower_gain, lower_weight = conv_block_backward(lower_gradient, token_states, lower_residuals, depthwise_kernels[0], block_norm_gains[0], pointwise_weights[0], token_valid_mask, LOWER_DILATION, False)
    return (jnp.stack([lower_kernel, upper_kernel]), jnp.stack([lower_gain, upper_gain]), jnp.stack([lower_weight, upper_weight]), grad_head)

def group_scores(goal_units, premise_units, positive):
    scores = logit_scale * lax.dot_general(goal_units, premise_units, (((1,), (1,)), ((), ())), preferred_element_type=jnp.float32)
    expon = jnp.exp(scores)
    total = lax.optimization_barrier(jnp.sum(expon, axis=1, keepdims=True))
    columns = jnp.arange(premise_units.shape[0], dtype=jnp.int32)
    onehot = (columns[None, :] == positive[:, None]).astype(jnp.float32)
    losses = jnp.log(total[:, 0]) - lax.optimization_barrier(jnp.sum(scores * onehot, axis=1))
    score_grad = ((expon / total - onehot) / G_DEV).astype(jnp.bfloat16)
    goal_grad = logit_scale * jnp.dot(score_grad, premise_units, preferred_element_type=jnp.float32)
    premise_grad = logit_scale * lax.dot_general(score_grad, goal_units, (((0,), (0,)), ((), ())), preferred_element_type=jnp.float32)
    return (losses, goal_grad, premise_grad)

def reference(goal_states, premise_states, goal_ids, premise_ids, positives, depthwise_kernels, block_norm_gains, pointwise_weights, head_weight):
    devices = N_REP * N_NEG
    token_states = jnp.concatenate([goal_states.reshape(devices, G_DEV, L, D), premise_states.reshape(devices, P_DEV, L, D)], axis=1)
    token_ids = jnp.concatenate([goal_ids.reshape(devices, G_DEV, L), premise_ids.reshape(devices, P_DEV, L)], axis=1)

    def forward_one(pair):
        return encode(pair[0], pair[1], depthwise_kernels, block_norm_gains, pointwise_weights, head_weight)[0]
    units = lax.map(forward_one, (token_states, token_ids))
    goal_units = units[:, :G_DEV].reshape(N_REP, GOALS_GRP, E)
    premise_units = units[:, G_DEV:].reshape(N_REP, PREM_GRP, E)
    losses, goal_grads, premise_grads = lax.map(lambda triple: group_scores(triple[0], triple[1], triple[2]), (goal_units, premise_units, positives))
    unit_grads = jnp.concatenate([goal_grads.reshape(devices, G_DEV, E), premise_grads.reshape(devices, P_DEV, E)], axis=1)
    initial = (jnp.zeros((2, K, D), jnp.float32), jnp.zeros((2, D), jnp.float32), jnp.zeros((2, D, D), jnp.float32), jnp.zeros((D, E), jnp.float32))

    def accumulate(totals, triple):
        terms = device_grads(triple[0], triple[1], triple[2], depthwise_kernels, block_norm_gains, pointwise_weights, head_weight)
        return (jax.tree.map(jnp.add, totals, terms), None)
    totals, ignored_value = lax.scan(accumulate, initial, (token_states, token_ids, unit_grads))
    return (losses, totals[0], totals[1], totals[2], totals[3])
```

```python
import jax
import jax.numpy as jnp
from jax import lax
from jax.sharding import PartitionSpec as P

LOWER_DILATION = 4
UPPER_DILATION = 8


N_NEG = 16
N_REP = 8
LANES = 128
logit_scale = 20.0


def to_rows(matrix):
    rows, columns = matrix.shape
    tiles = matrix.reshape(rows // 8, 8, columns // LANES, LANES)
    return tiles.transpose(0, 2, 1, 3).reshape(rows * columns // LANES, LANES)


def from_rows(flat, shape):
    rows, columns = shape
    tiles = flat.reshape(rows // 8, columns // LANES, 8, LANES)
    return tiles.transpose(0, 2, 1, 3).reshape(rows, columns)


def reduce_everywhere(arrays):
    devices = N_NEG * N_REP
    flat = [to_rows(array.astype(jnp.bfloat16)) for array in arrays]
    used = sum(piece.shape[0] for piece in flat)
    slice_rows = -(-used // (devices * 8)) * 8
    flat.append(jnp.zeros((devices * slice_rows - used, LANES), jnp.bfloat16))
    packed = jnp.concatenate(flat, axis=0).reshape(devices, slice_rows, LANES)
    axes = ("neg", "rep")
    received = lax.all_to_all(packed, axes, 0, 0)
    own = jnp.sum(received.astype(jnp.float32), axis=0).astype(jnp.bfloat16)
    spread = lax.all_to_all(
        jnp.broadcast_to(own[None], (devices, slice_rows, LANES)), axes, 0, 0
    )
    rows = spread.reshape(devices * slice_rows, LANES)
    results, start = [], 0
    for array in arrays:
        count = array.size // LANES
        piece = rows[start : start + count]
        results.append(from_rows(piece, array.shape).astype(jnp.float32))
        start += count
    return results


def shift_down(values, dilation):
    return jnp.pad(values, ((0, 0), (dilation, 0), (0, 0)))[:, : values.shape[1]]


def shift_up(values, dilation):
    return jnp.pad(values, ((0, 0), (0, dilation), (0, 0)))[:, dilation:]


def depth_conv(inputs, kernel, dilation):
    return (
        kernel[0] * shift_down(inputs, dilation)
        + kernel[1] * inputs
        + kernel[2] * shift_up(inputs, dilation)
    )


def conv_block_forward(hidden, kernel, gain, weight, token_valid_mask, dilation):
    widened = hidden.astype(jnp.float32)
    inverse = lax.rsqrt(jnp.mean(widened * widened, axis=-1, keepdims=True) + 1e-06)
    normed = widened * inverse * gain * token_valid_mask
    mixed = depth_conv(normed, kernel, dilation).astype(jnp.bfloat16)
    count, length, width = hidden.shape
    pre_act = jnp.dot(
        mixed.reshape(count * length, width), weight, preferred_element_type=jnp.float32
    ).reshape(count, length, width)
    output = (widened + jax.nn.gelu(pre_act, approximate=True)).astype(jnp.bfloat16)
    return (output, (inverse, mixed, pre_act))


def conv_block_backward(
    upstream, hidden, saved, kernel, gain, weight, token_valid_mask, dilation, need_input
):
    inverse, mixed, pre_act = saved
    widened = hidden.astype(jnp.float32)
    normed = widened * inverse * gain * token_valid_mask
    ignored_value, gelu_back = jax.vjp(lambda value: jax.nn.gelu(value, approximate=True), pre_act)
    act_grad = gelu_back(upstream)[0].astype(jnp.bfloat16)
    count, length, width = hidden.shape
    flat_grad = act_grad.reshape(count * length, width)
    grad_weight = jnp.dot(
        mixed.reshape(count * length, width).T, flat_grad, preferred_element_type=jnp.float32
    )
    conv_grad = jnp.dot(flat_grad, weight.T, preferred_element_type=jnp.float32).reshape(
        count, length, width
    )
    grad_kernel = jnp.stack(
        [
            jnp.sum(shift_down(normed, dilation) * conv_grad, axis=(0, 1)),
            jnp.sum(normed * conv_grad, axis=(0, 1)),
            jnp.sum(shift_up(normed, dilation) * conv_grad, axis=(0, 1)),
        ]
    )
    normed_grad = (
        kernel[0] * shift_up(conv_grad, dilation)
        + kernel[1] * conv_grad
        + kernel[2] * shift_down(conv_grad, dilation)
    ) * token_valid_mask
    grad_gain = jnp.sum(normed_grad * widened * inverse, axis=(0, 1))
    input_grad = None
    if need_input:
        scaled = normed_grad * gain
        input_grad = (
            upstream
            + inverse * scaled
            - widened * inverse**3 * jnp.mean(scaled * widened, axis=-1, keepdims=True)
        )
    return (input_grad, grad_kernel, grad_gain, grad_weight)


def pool_forward(hidden, token_valid_mask, head_weight):
    widened = hidden.astype(jnp.float32)
    counts = jnp.sum(token_valid_mask, axis=1)
    pooled = (jnp.sum(widened * token_valid_mask, axis=1) / counts).astype(jnp.bfloat16)
    embedded = jnp.dot(pooled, head_weight, preferred_element_type=jnp.float32)
    magnitude = jnp.sqrt(jnp.sum(embedded * embedded, axis=-1, keepdims=True) + 1e-06)
    unit = embedded / magnitude
    return (unit.astype(jnp.bfloat16), (counts, pooled, unit, magnitude))


def pool_backward(unit_grad, saved, token_valid_mask, head_weight):
    counts, pooled, unit, magnitude = saved
    embed_grad = (
        (unit_grad - unit * jnp.sum(unit * unit_grad, axis=-1, keepdims=True)) / magnitude
    ).astype(jnp.bfloat16)
    grad_head = jnp.dot(pooled.T, embed_grad, preferred_element_type=jnp.float32)
    pooled_grad = jnp.dot(embed_grad, head_weight.T, preferred_element_type=jnp.float32)
    hidden_gradient = (pooled_grad / counts)[:, None, :] * token_valid_mask
    return (hidden_gradient, grad_head)


def local(
    goal_states,
    premise_states,
    goal_ids,
    premise_ids,
    positives,
    depthwise_kernels,
    block_norm_gains,
    pointwise_weights,
    head_weight,
):
    goal_count = goal_states.shape[1]
    token_states = jnp.concatenate([goal_states[0], premise_states[0]], axis=0)
    token_ids = jnp.concatenate([goal_ids[0], premise_ids[0]], axis=0)
    token_valid_mask = (token_ids != 0).astype(jnp.float32)[..., None]
    first_hidden, lower_residuals = conv_block_forward(
        token_states,
        depthwise_kernels[0],
        block_norm_gains[0],
        pointwise_weights[0],
        token_valid_mask,
        LOWER_DILATION,
    )
    second_hidden, upper_residuals = conv_block_forward(
        first_hidden,
        depthwise_kernels[1],
        block_norm_gains[1],
        pointwise_weights[1],
        token_valid_mask,
        UPPER_DILATION,
    )
    units, saved_pool = pool_forward(second_hidden, token_valid_mask, head_weight)
    goal_units = units[:goal_count]
    premise_units = units[goal_count:]
    group_positive = positives[0]
    position = lax.axis_index("neg")
    gathered = lax.all_to_all(
        jnp.broadcast_to(units[None], (N_NEG,) + units.shape), "neg", 0, 0
    )
    group_goals = gathered[:, :goal_count].reshape(N_NEG * goal_count, -1)
    group_premises = gathered[:, goal_count:].reshape(-1, units.shape[1])
    premise_count = units.shape[0] - goal_count
    scores = logit_scale * lax.dot_general(
        group_goals, group_premises, (((1,), (1,)), ((), ())), preferred_element_type=jnp.float32
    )
    expon = jnp.exp(scores)
    total = jnp.sum(expon, axis=1, keepdims=True)
    columns = jnp.arange(group_premises.shape[0], dtype=jnp.int32)
    onehot = (columns[None, :] == group_positive[:, None]).astype(jnp.float32)
    group_losses = jnp.log(total[:, 0]) - jnp.sum(scores * onehot, axis=1)
    losses = lax.dynamic_slice_in_dim(group_losses, position * goal_count, goal_count)
    score_grad = ((expon / total - onehot) / goal_count).astype(jnp.bfloat16)
    own_rows = lax.dynamic_slice_in_dim(score_grad, position * goal_count, goal_count, 0)
    own_columns = lax.dynamic_slice_in_dim(
        score_grad, position * premise_count, premise_count, 1
    )
    goal_grad = logit_scale * jnp.dot(
        own_rows, group_premises, preferred_element_type=jnp.float32
    )
    premise_grad = logit_scale * lax.dot_general(
        own_columns, group_goals, (((0,), (0,)), ((), ())), preferred_element_type=jnp.float32
    )
    unit_grad = jnp.concatenate([goal_grad, premise_grad], axis=0)
    hidden_gradient, grad_head = pool_backward(unit_grad, saved_pool, token_valid_mask, head_weight)
    lower_gradient, upper_kernel, upper_gain, upper_weight = conv_block_backward(
        hidden_gradient,
        first_hidden,
        upper_residuals,
        depthwise_kernels[1],
        block_norm_gains[1],
        pointwise_weights[1],
        token_valid_mask,
        UPPER_DILATION,
        True,
    )
    ignored_value, lower_kernel, lower_gain, lower_weight = conv_block_backward(
        lower_gradient,
        token_states,
        lower_residuals,
        depthwise_kernels[0],
        block_norm_gains[0],
        pointwise_weights[0],
        token_valid_mask,
        LOWER_DILATION,
        False,
    )
    sums = reduce_everywhere(
        [
            lower_weight,
            upper_weight,
            grad_head,
            jnp.concatenate(
                [lower_kernel, upper_kernel, lower_gain[None], upper_gain[None]], axis=0
            ),
        ]
    )
    weights = jnp.stack(sums[:2])
    small = sums[3]
    return (
        losses[None, :],
        small[:6].reshape(2, 3, -1),
        small[6:8],
        weights,
        sums[2],
    )


def solution(mesh):
    placed = (
        P("rep", "neg", None, None),
        P("rep", "neg", None, None),
        P("rep", "neg", None),
        P("rep", "neg", None),
        P("rep", None),
        P(),
        P(),
        P(),
        P(),
    )
    return jax.shard_map(
        local,
        mesh=mesh,
        in_specs=placed,
        out_specs=(P("rep", "neg"), P(), P(), P(), P()),
        check_vma=False,
    )
```

```python
import functools

import jax
import jax.numpy as jnp
from jax import lax
from jax.experimental import pallas as pl
from jax.experimental.pallas import tpu as pltpu
from jax.sharding import PartitionSpec as P

LOWER_DILATION = 4
UPPER_DILATION = 8
N_NEG = 16
N_REP = 8
LANES = 128
PAD = 8
TILE = 16
SEQS = 4
EPS = 1e-06
GELU_C = 0.7978845608028654
GELU_A = 0.044715
logit_scale = 20.0
F32 = jnp.float32
BF16 = jnp.bfloat16


def gelu_parts(x):
    square = x * x
    half = 0.5 + 0.5 * jnp.tanh(x * (GELU_C + (GELU_C * GELU_A) * square))
    value = x * half
    slope = half + value * (1.0 - half) * (
        2.0 * GELU_C + (6.0 * GELU_C * GELU_A) * square
    )
    return value, slope


def forward_kernel(
    lengths,
    goal_ref,
    premise_ref,
    mix_gain_ref,
    weight_ref,
    head_ref,
    shifted_ref,
    slope_low_ref,
    normed_up_ref,
    mixed_up_ref,
    slope_up_ref,
    inverse_ref,
    pooled_ref,
    unit_ref,
    magnitude_ref,
    spread_ref,
    states,
    padded,
    mixed,
    pre_act,
    hidden,
):
    step = pl.program_id(0)
    length, width = states.shape[1], states.shape[2]
    tiles = range(0, length, TILE)
    rows = lax.broadcasted_iota(jnp.int32, (TILE, 1), 0)

    @pl.when(step == 0)
    def _():
        zeros = jnp.zeros((SEQS, PAD, width), F32)
        padded[:, :PAD, :] = zeros
        padded[:, PAD + length :, :] = zeros

    def norm(values, valid):
        mean = jnp.mean(values * values, axis=-1, keepdims=True)
        inverse = jnp.where(valid, lax.rsqrt(mean + EPS), 0.0)
        return values * inverse, inverse

    def norm_inputs(source):
        def body(seq, carry):
            count = lengths[step * SEQS + seq]
            for start in tiles:
                raw = source[0, seq, pl.ds(start, TILE), :]
                states[seq, pl.ds(start, TILE), :] = raw
                normed, _ = norm(raw.astype(F32), rows < count - start)
                padded[seq, pl.ds(PAD + start, TILE), :] = normed
            return carry

        lax.fori_loop(0, SEQS, body, 0)

    goal_steps = goal_total // SEQS

    @pl.when(step < goal_steps)
    def _():
        norm_inputs(goal_ref)

    @pl.when(step >= goal_steps)
    def _():
        norm_inputs(premise_ref)

    def mix_low(seq, carry):
        for start in tiles:
            window = [
                padded[seq, pl.ds(PAD + start + tap * LOWER_DILATION, TILE), :]
                for tap in (-1, 0, 1)
            ]
            total = 0.0
            for tap in range(3):
                total = total + mix_gain_ref[0, tap : tap + 1, :] * window[tap]
                shifted_ref[seq, pl.ds(start, TILE), tap * width : (tap + 1) * width] = (
                    window[tap].astype(BF16)
                )
            mixed[seq, pl.ds(start, TILE), :] = total.astype(BF16)
        return carry

    lax.fori_loop(0, SEQS, mix_low, 0)
    pre_act[...] = jnp.dot(
        mixed[...].reshape(SEQS * length, width), weight_ref[0], preferred_element_type=F32
    ).reshape(SEQS, length, width)

    def act_low(seq, carry):
        count = lengths[step * SEQS + seq]
        for start in tiles:
            at = pl.ds(start, TILE)
            value, slope = gelu_parts(pre_act[seq, at, :])
            slope_low_ref[seq, at, :] = slope.astype(BF16)
            out = states[seq, at, :].astype(F32) + value
            hidden[seq, at, :] = out
            normed, inverse = norm(out, rows < count - start)
            padded[seq, pl.ds(PAD + start, TILE), :] = normed
            normed_up_ref[seq, at, :] = normed.astype(BF16)
            inverse_ref[seq, at, :] = jnp.broadcast_to(inverse, (TILE, LANES))
        return carry

    lax.fori_loop(0, SEQS, act_low, 0)

    def mix_up(seq, carry):
        for start in tiles:
            at = pl.ds(start, TILE)
            total = 0.0
            for tap in range(3):
                total = total + mix_gain_ref[1, tap : tap + 1, :] * (
                    padded[seq, pl.ds(PAD + start + (tap - 1) * UPPER_DILATION, TILE), :]
                )
            mixed_up_ref[seq, at, :] = total.astype(BF16)
        return carry

    lax.fori_loop(0, SEQS, mix_up, 0)
    pre_act[...] = jnp.dot(
        mixed_up_ref[...].reshape(SEQS * length, width),
        weight_ref[1],
        preferred_element_type=F32,
    ).reshape(SEQS, length, width)

    def act_up(seq, carry):
        count = lengths[step * SEQS + seq]
        pooled = jnp.zeros((TILE, width), F32)
        for start in tiles:
            at = pl.ds(start, TILE)
            valid = rows < count - start
            value, slope = gelu_parts(pre_act[seq, at, :])
            slope_up_ref[seq, at, :] = jnp.where(valid, slope, 0.0).astype(BF16)
            pooled = pooled + jnp.where(valid, hidden[seq, at, :] + value, 0.0)
        pooled_ref[pl.ds(step * SEQS + seq, 1), :] = (
            jnp.sum(pooled, axis=0, keepdims=True) / count.astype(F32)
        )
        return carry

    lax.fori_loop(0, SEQS, act_up, 0)

    @pl.when(step == pl.num_programs(0) - 1)
    def _():
        embedded = jnp.dot(
            pooled_ref[...].astype(BF16), head_ref[...], preferred_element_type=F32
        )
        magnitude = jnp.sqrt(jnp.sum(embedded * embedded, axis=-1, keepdims=True) + EPS)
        unit = embedded / magnitude
        unit_ref[...] = unit
        magnitude_ref[...] = jnp.broadcast_to(magnitude, magnitude_ref.shape)
        rounded = unit.astype(BF16)
        for peer in range(N_NEG):
            spread_ref[peer] = rounded


def backward_kernel(
    lengths,
    gathered_ref,
    own_unit_ref,
    unit_ref,
    magnitude_ref,
    pooled_ref,
    own_target_ref,
    own_index_ref,
    own_count_ref,
    column_target_ref,
    head_ref,
    mix_gain_ref,
    weight_ref,
    weight_turned_ref,
    shifted_ref,
    slope_low_ref,
    normed_up_ref,
    mixed_up_ref,
    slope_up_ref,
    inverse_ref,
    loss_ref,
    head_grad_ref,
    point_up_ref,
    corr_up_ref,
    point_low_ref,
    corr_low_ref,
    upstream,
    act_grad,
    conv_grad,
    corr,
    point_up,
    moments,
):
    step = pl.program_id(0)
    last = pl.num_programs(0) - 1
    length, width = act_grad.shape[1], act_grad.shape[2]
    tiles = range(0, length, TILE)

    @pl.when(step == 0)
    def _():
        zeros = jnp.zeros((SEQS, PAD, width), F32)
        conv_grad[:, :PAD, :] = zeros
        conv_grad[:, PAD + length :, :] = zeros
        corr[...] = jnp.zeros_like(corr)
        point_up[...] = jnp.zeros_like(point_up)
        moments[...] = jnp.zeros_like(moments)
        every = gathered_ref[...]
        total_count = every.shape[0]
        own_count = own_unit_ref.shape[0]
        contract = (((1,), (1,)), ((), ()))
        gram = lax.dot_general(every, every, contract, preferred_element_type=F32)
        row_of = lax.broadcasted_iota(jnp.int32, (total_count, 1), 0)
        row_goal = lax.rem(row_of, own_count) < goal_total
        expon = jnp.where(row_goal, 0.0, jnp.exp(logit_scale * gram))
        column_total = jnp.sum(expon, axis=0, keepdims=True)
        scores = logit_scale * lax.dot_general(
            own_unit_ref[...], every, contract, preferred_element_type=F32
        )
        own_expon = jnp.exp(scores)
        column_of = lax.broadcasted_iota(jnp.int32, (own_count, total_count), 1)
        column_goal = lax.rem(column_of, own_count) < goal_total
        own_goal = lax.broadcasted_iota(jnp.int32, (own_count, total_count), 0) < goal_total
        own_total = jnp.sum(
            jnp.where(column_goal, 0.0, own_expon), axis=1, keepdims=True
        )
        hit_goal = column_of == own_target_ref[...]
        hit_premise = column_target_ref[...] == own_index_ref[...]
        of_goal = own_expon / own_total - jnp.where(hit_goal, 1.0, 0.0)
        of_premise = own_expon / column_total - jnp.where(hit_premise, 1.0, 0.0)
        score_grad = jnp.where(
            own_goal,
            jnp.where(column_goal, 0.0, of_goal),
            jnp.where(column_goal, of_premise, 0.0),
        )
        score_grad = (score_grad / float(goal_total)).astype(BF16)
        chosen = jnp.sum(jnp.where(hit_goal, scores, 0.0), axis=1, keepdims=True)
        loss_ref[...] = jnp.broadcast_to(jnp.log(own_total) - chosen, loss_ref.shape)
        unit_grad = logit_scale * jnp.dot(score_grad, every, preferred_element_type=F32)
        unit = unit_ref[...]
        along = jnp.sum(unit * unit_grad, axis=-1, keepdims=True)
        embed_grad = ((unit_grad - unit * along) / magnitude_ref[:, :1]).astype(BF16)
        head_grad_ref[...] = lax.dot_general(
            pooled_ref[...].astype(BF16),
            embed_grad,
            (((0,), (0,)), ((), ())),
            preferred_element_type=F32,
        ).astype(head_grad_ref.dtype)
        pooled_grad = lax.dot_general(
            embed_grad, head_ref[...], contract, preferred_element_type=F32
        )
        upstream[...] = pooled_grad / own_count_ref[:, :1]

    def grad_up(seq, carry):
        above = upstream[pl.ds(step * SEQS + seq, 1), :]
        for start in tiles:
            at = pl.ds(start, TILE)
            act_grad[seq, at, :] = (slope_up_ref[seq, at, :].astype(F32) * above).astype(BF16)
        return carry

    lax.fori_loop(0, SEQS, grad_up, 0)
    flat = act_grad[...].reshape(SEQS * length, width)
    conv_grad[:, PAD : PAD + length, :] = lax.dot_general(
        flat, weight_ref[1], (((1,), (1,)), ((), ())), preferred_element_type=F32
    ).reshape(SEQS, length, width)
    over_tokens = (((0,), (0,)), ((), ()))
    point_up[...] += lax.dot_general(
        mixed_up_ref[...].reshape(SEQS * length, width),
        flat,
        over_tokens,
        preferred_element_type=F32,
    )

    def norm_up(seq, carry):
        above = upstream[pl.ds(step * SEQS + seq, 1), :]
        sums = [corr[tap] for tap in range(3)]
        for start in tiles:
            at = pl.ds(start, TILE)
            normed = normed_up_ref[seq, at, :].astype(F32)
            inverse = inverse_ref[seq, at, :][:, :1]
            scaled = 0.0
            for tap in range(3):
                part = conv_grad[seq, pl.ds(PAD + start + (1 - tap) * UPPER_DILATION, TILE), :]
                scaled = scaled + mix_gain_ref[1, tap : tap + 1, :] * part
                product = part * normed
                sums[tap] = sums[tap] + product[:8] + product[8:]
            mean = jnp.mean(scaled * normed, axis=-1, keepdims=True)
            below = jnp.where(inverse > 0.0, above, 0.0) + inverse * (scaled - normed * mean)
            act_grad[seq, at, :] = (below * slope_low_ref[seq, at, :].astype(F32)).astype(BF16)
        for tap in range(3):
            corr[tap] = sums[tap]
        return carry

    lax.fori_loop(0, SEQS, norm_up, 0)
    moments[...] += lax.dot_general(
        act_grad[...].reshape(SEQS * length, width),
        shifted_ref[...].reshape(SEQS * length, 3 * width),
        over_tokens,
        preferred_element_type=F32,
    )

    @pl.when(step == last)
    def _():
        point_up_ref[...] = point_up[...].astype(point_up_ref.dtype)
        point = 0.0
        for tap in range(3):
            corr_up_ref[tap : tap + 1, :] = jnp.sum(corr[tap], axis=0, keepdims=True)
            part = moments[:, tap * width : (tap + 1) * width]
            corr_low_ref[tap : tap + 1, :] = jnp.sum(
                part * weight_turned_ref[...].astype(F32), axis=0, keepdims=True
            )
            point = point + mix_gain_ref[0, tap : tap + 1, :] * part
        point_low_ref[...] = point.T.astype(point_low_ref.dtype)


goal_total = 8


def whole(shape):
    return pl.BlockSpec(shape, lambda i, *_: (0,) * len(shape))


def chunk(length, width):
    return pl.BlockSpec((SEQS, length, width), lambda i, *_: (i, 0, 0))


def run_forward(goal_states, premise_states, lengths, mix_gain, weights, head_weight):
    goals, length, width = goal_states.shape[1:]
    premises = premise_states.shape[1]
    count = goals + premises
    embed = head_weight.shape[1]
    goal_steps = goals // SEQS
    tokens = lambda w, t: jax.ShapeDtypeStruct((count, length, w), t)
    outs = [
        (tokens(3 * width, BF16), chunk(length, 3 * width)),
        (tokens(width, BF16), chunk(length, width)),
        (tokens(width, BF16), chunk(length, width)),
        (tokens(width, BF16), chunk(length, width)),
        (tokens(width, BF16), chunk(length, width)),
        (tokens(LANES, F32), chunk(length, LANES)),
        (jax.ShapeDtypeStruct((count, width), F32), whole((count, width))),
        (jax.ShapeDtypeStruct((count, embed), F32), whole((count, embed))),
        (jax.ShapeDtypeStruct((count, LANES), F32), whole((count, LANES))),
        (
            jax.ShapeDtypeStruct((N_NEG, count, embed), BF16),
            whole((N_NEG, count, embed)),
        ),
    ]
    return pl.pallas_call(
        forward_kernel,
        name="forward",
        out_shape=[o[0] for o in outs],
        grid_spec=pltpu.PrefetchScalarGridSpec(
            num_scalar_prefetch=1,
            grid=(count // SEQS,),
            in_specs=[
                pl.BlockSpec(
                    (1, SEQS, length, width),
                    lambda i, *_: (0, jnp.minimum(i, goal_steps - 1), 0, 0),
                ),
                pl.BlockSpec(
                    (1, SEQS, length, width),
                    lambda i, *_: (0, jnp.maximum(i - goal_steps, 0), 0, 0),
                ),
                whole(mix_gain.shape),
                whole(weights.shape),
                whole(head_weight.shape),
            ],
            out_specs=[o[1] for o in outs],
            scratch_shapes=[
                pltpu.VMEM((SEQS, length, width), BF16),
                pltpu.VMEM((SEQS, length + 2 * PAD, width), F32),
                pltpu.VMEM((SEQS, length, width), BF16),
                pltpu.VMEM((SEQS, length, width), F32),
                pltpu.VMEM((SEQS, length, width), F32),
            ],
        ),
        compiler_params=pltpu.CompilerParams(
            dimension_semantics=("arbitrary",), vmem_limit_bytes=50 << 20
        ),
    )(lengths, goal_states, premise_states, mix_gain, weights, head_weight)


def run_backward(lengths, tables, head_weight, mix_gain, weights, turned, residuals):
    count, length, width = residuals[1].shape
    embed = head_weight.shape[1]
    singles = list(tables) + [head_weight, mix_gain, weights, turned]
    outs = [
        jax.ShapeDtypeStruct((count, LANES), F32),
        jax.ShapeDtypeStruct((width, embed), BF16),
        jax.ShapeDtypeStruct((width, width), BF16),
        jax.ShapeDtypeStruct((3, width), F32),
        jax.ShapeDtypeStruct((width, width), BF16),
        jax.ShapeDtypeStruct((3, width), F32),
    ]
    return pl.pallas_call(
        backward_kernel,
        name="backward",
        out_shape=outs,
        grid_spec=pltpu.PrefetchScalarGridSpec(
            num_scalar_prefetch=1,
            grid=(count // SEQS,),
            in_specs=[whole(s.shape) for s in singles]
            + [chunk(length, r.shape[2]) for r in residuals],
            out_specs=[whole(o.shape) for o in outs],
            scratch_shapes=[
                pltpu.VMEM((count, width), F32),
                pltpu.VMEM((SEQS, length, width), BF16),
                pltpu.VMEM((SEQS, length + 2 * PAD, width), F32),
                pltpu.VMEM((3, 8, width), F32),
                pltpu.VMEM((width, width), F32),
                pltpu.VMEM((width, 3 * width), F32),
            ],
        ),
        compiler_params=pltpu.CompilerParams(
            dimension_semantics=("arbitrary",), vmem_limit_bytes=50 << 20
        ),
    )(lengths, *singles, *residuals)


def to_rows(matrix):
    rows, columns = matrix.shape
    tiles = matrix.reshape(rows // 8, 8, columns // LANES, LANES)
    return tiles.transpose(0, 2, 1, 3).reshape(rows * columns // LANES, LANES)


def from_rows(flat, shape):
    rows, columns = shape
    tiles = flat.reshape(rows // 8, columns // LANES, 8, LANES)
    return tiles.transpose(0, 2, 1, 3).reshape(rows, columns)


def reduce_everywhere(arrays):
    devices = N_NEG * N_REP
    flat = [to_rows(array.astype(jnp.bfloat16)) for array in arrays]
    used = sum(piece.shape[0] for piece in flat)
    slice_rows = -(-used // (devices * 8)) * 8
    flat.append(jnp.zeros((devices * slice_rows - used, LANES), jnp.bfloat16))
    packed = jnp.concatenate(flat, axis=0).reshape(devices, slice_rows, LANES)
    axes = ("neg", "rep")
    received = lax.all_to_all(packed, axes, 0, 0)
    own = jnp.sum(received.astype(jnp.float32), axis=0).astype(jnp.bfloat16)
    spread = lax.all_to_all(
        jnp.broadcast_to(own[None], (devices, slice_rows, LANES)), axes, 0, 0
    )
    rows = spread.reshape(devices * slice_rows, LANES)
    results, start = [], 0
    for array in arrays:
        count = array.size // LANES
        piece = rows[start : start + count]
        results.append(from_rows(piece, array.shape).astype(jnp.float32))
        start += count
    return results


def local(
    goal_states,
    premise_states,
    goal_ids,
    premise_ids,
    positives,
    depthwise_kernels,
    block_norm_gains,
    pointwise_weights,
    head_weight,
):
    goals = goal_states.shape[1]
    premises = premise_states.shape[1]
    count = goals + premises
    lengths = jnp.sum(
        (jnp.concatenate([goal_ids[0], premise_ids[0]], axis=0) != 0).astype(jnp.int32), axis=1
    )
    mix_gain = depthwise_kernels * block_norm_gains[:, None, :]
    outs = run_forward(
        goal_states, premise_states, lengths, mix_gain, pointwise_weights, head_weight
    )
    residuals, (pooled, unit, magnitude, spread) = outs[:6], outs[6:]
    gathered = lax.all_to_all(spread, "neg", 0, 0).reshape(N_NEG * count, -1)
    position = lax.axis_index("neg")
    slot = positives[0] // premises * count + goals + positives[0] % premises
    slot = jnp.concatenate(
        [
            slot.reshape(N_NEG, goals).astype(jnp.int32),
            jnp.full((N_NEG, premises), -1, jnp.int32),
        ],
        axis=1,
    )
    own_target = lax.dynamic_slice_in_dim(slot, position, 1, 0).reshape(count, 1)
    own_index = (position * count + jnp.arange(count, dtype=jnp.int32)).reshape(count, 1)
    own_count = lengths.astype(F32).reshape(count, 1)
    tables = (
        gathered,
        spread[0],
        unit,
        magnitude,
        pooled,
        own_target,
        own_index,
        own_count,
        slot.reshape(1, N_NEG * count),
    )
    loss, head_grad, point_up, corr_up, point_low, corr_low = run_backward(
        lengths,
        tables,
        head_weight,
        mix_gain,
        pointwise_weights,
        pointwise_weights[0].T,
        residuals,
    )
    corr = jnp.stack([corr_low, corr_up])
    kernel_grad = corr * block_norm_gains[:, None, :]
    gain_grad = jnp.sum(corr * depthwise_kernels, axis=1)
    sums = reduce_everywhere(
        [
            point_low,
            point_up,
            head_grad,
            jnp.concatenate([kernel_grad.reshape(6, -1), gain_grad], axis=0),
        ]
    )
    small = sums[3]
    return (
        loss[:goals, 0][None, :],
        small[:6].reshape(2, 3, -1),
        small[6:8],
        jnp.stack(sums[:2]),
        sums[2],
    )


def solution(mesh):
    placed = (
        P("rep", "neg", None, None),
        P("rep", "neg", None, None),
        P("rep", "neg", None),
        P("rep", "neg", None),
        P("rep", None),
        P(),
        P(),
        P(),
        P(),
    )
    return jax.shard_map(
        local,
        mesh=mesh,
        in_specs=placed,
        out_specs=(P("rep", "neg"), P(), P(), P(), P()),
        check_vma=False,
    )
```

```python
import functools

import jax
import jax.numpy as jnp
from jax import lax
from jax.experimental import pallas as pl
from jax.experimental.pallas import tpu as pltpu
from jax.sharding import Mesh
from jax.sharding import PartitionSpec as P

LOWER_DILATION = 4
UPPER_DILATION = 8
N_NEG = 16
N_REP = 8
LANES = 128
PAD = 8
TILE = 16
SEQS = 4
SLICE = 48
EPS = 1e-06
GELU_C = 0.7978845608028654
GELU_A = 0.044715
logit_scale = 20.0
F32 = jnp.float32
BF16 = jnp.bfloat16


def gelu_parts(x):
    square = x * x
    half = 0.5 + 0.5 * jnp.tanh(x * (GELU_C + (GELU_C * GELU_A) * square))
    value = x * half
    slope = half + value * (1.0 - half) * (
        2.0 * GELU_C + (6.0 * GELU_C * GELU_A) * square
    )
    return value, slope


def forward_kernel(
    lengths,
    goal_ref,
    premise_ref,
    depth_ref,
    gain_ref,
    weight_ref,
    head_ref,
    shifted_ref,
    slope_low_ref,
    normed_up_ref,
    mixed_up_ref,
    slope_up_ref,
    inverse_ref,
    summary_ref,
    spread_ref,
    states,
    padded,
    mixed,
    pre_act,
    hidden,
    mix_gain,
):
    step = pl.program_id(0)
    length, width = states.shape[1], states.shape[2]
    tiles = range(0, length, TILE)
    rows = lax.broadcasted_iota(jnp.int32, (TILE, 1), 0)

    @pl.when(step == 0)
    def _():
        zeros = jnp.zeros((SEQS, PAD, width), F32)
        padded[:, :PAD, :] = zeros
        padded[:, PAD + length :, :] = zeros
        mix_gain[...] = depth_ref[...] * gain_ref[...]

    def norm(values, valid):
        mean = jnp.mean(values * values, axis=-1, keepdims=True)
        inverse = jnp.where(valid, lax.rsqrt(mean + EPS), 0.0)
        return values * inverse, inverse

    def norm_inputs(source):
        def body(seq, carry):
            count = lengths[step * SEQS + seq]
            for start in tiles:
                raw = source[0, seq, pl.ds(start, TILE), :]
                states[seq, pl.ds(start, TILE), :] = raw
                normed, _ = norm(raw.astype(F32), rows < count - start)
                padded[seq, pl.ds(PAD + start, TILE), :] = normed
            return carry

        lax.fori_loop(0, SEQS, body, 0)

    goal_steps = goal_total // SEQS

    @pl.when(step < goal_steps)
    def _():
        norm_inputs(goal_ref)

    @pl.when(step >= goal_steps)
    def _():
        norm_inputs(premise_ref)

    def mix_low(seq, carry):
        for start in tiles:
            window = [
                padded[seq, pl.ds(PAD + start + tap * LOWER_DILATION, TILE), :]
                for tap in (-1, 0, 1)
            ]
            total = 0.0
            for tap in range(3):
                total = total + mix_gain[tap, 0:1, :] * window[tap]
                shifted_ref[seq, pl.ds(start, TILE), tap * width : (tap + 1) * width] = (
                    window[tap].astype(BF16)
                )
            mixed[seq, pl.ds(start, TILE), :] = total.astype(BF16)
        return carry

    lax.fori_loop(0, SEQS, mix_low, 0)
    pre_act[...] = jnp.dot(
        mixed[...].reshape(SEQS * length, width), weight_ref[0], preferred_element_type=F32
    ).reshape(SEQS, length, width)

    def act_low(seq, carry):
        count = lengths[step * SEQS + seq]
        for start in tiles:
            at = pl.ds(start, TILE)
            value, slope = gelu_parts(pre_act[seq, at, :])
            slope_low_ref[seq, at, :] = slope.astype(BF16)
            out = states[seq, at, :].astype(F32) + value
            hidden[seq, at, :] = out
            normed, inverse = norm(out, rows < count - start)
            padded[seq, pl.ds(PAD + start, TILE), :] = normed
            normed_up_ref[seq, at, :] = normed.astype(BF16)
            inverse_ref[seq, at, :] = jnp.broadcast_to(inverse, (TILE, LANES))
        return carry

    lax.fori_loop(0, SEQS, act_low, 0)

    def mix_up(seq, carry):
        for start in tiles:
            at = pl.ds(start, TILE)
            total = 0.0
            for tap in range(3):
                total = total + mix_gain[tap, 1:2, :] * (
                    padded[seq, pl.ds(PAD + start + (tap - 1) * UPPER_DILATION, TILE), :]
                )
            mixed_up_ref[seq, at, :] = total.astype(BF16)
        return carry

    lax.fori_loop(0, SEQS, mix_up, 0)
    pre_act[...] = jnp.dot(
        mixed_up_ref[...].reshape(SEQS * length, width),
        weight_ref[1],
        preferred_element_type=F32,
    ).reshape(SEQS, length, width)

    def act_up(seq, carry):
        count = lengths[step * SEQS + seq]
        pooled = jnp.zeros((TILE, width), F32)
        for start in tiles:
            at = pl.ds(start, TILE)
            valid = rows < count - start
            value, slope = gelu_parts(pre_act[seq, at, :])
            slope_up_ref[seq, at, :] = jnp.where(valid, slope, 0.0).astype(BF16)
            pooled = pooled + jnp.where(valid, hidden[seq, at, :] + value, 0.0)
        summary_ref[pl.ds(step * SEQS + seq, 1), :width] = (
            jnp.sum(pooled, axis=0, keepdims=True) / count.astype(F32)
        )
        return carry

    lax.fori_loop(0, SEQS, act_up, 0)

    @pl.when(step == pl.num_programs(0) - 1)
    def _():
        embedded = jnp.dot(
            summary_ref[:, :width].astype(BF16), head_ref[...], preferred_element_type=F32
        )
        magnitude = jnp.sqrt(jnp.sum(embedded * embedded, axis=-1, keepdims=True) + EPS)
        unit = embedded / magnitude
        embed = unit.shape[1]
        summary_ref[:, width : width + embed] = unit
        summary_ref[:, width + embed :] = jnp.broadcast_to(magnitude, (unit.shape[0], LANES))
        rounded = unit.astype(BF16)
        for peer in range(N_NEG):
            spread_ref[peer] = rounded


def backward_kernel(
    scalars,
    gathered_ref,
    summary_ref,
    column_target_ref,
    head_ref,
    depth_ref,
    gain_ref,
    weight_ref,
    weight_turned_ref,
    shifted_ref,
    slope_low_ref,
    normed_up_ref,
    mixed_up_ref,
    slope_up_ref,
    inverse_ref,
    loss_ref,
    keep_ref,
    send_ref,
    upstream,
    act_grad,
    conv_grad,
    corr,
    point_up,
    moments,
    head_grad,
    mix_gain,
):
    step = pl.program_id(0)
    last = pl.num_programs(0) - 1
    count = summary_ref.shape[0]
    position, core = scalars[count], scalars[count + 1]
    length, width = act_grad.shape[1], act_grad.shape[2]
    tiles = range(0, length, TILE)

    @pl.when(step == 0)
    def _():
        zeros = jnp.zeros((SEQS, PAD, width), F32)
        conv_grad[:, :PAD, :] = zeros
        conv_grad[:, PAD + length :, :] = zeros
        corr[...] = jnp.zeros_like(corr)
        point_up[...] = jnp.zeros_like(point_up)
        moments[...] = jnp.zeros_like(moments)
        every = gathered_ref[...]
        total_count = every.shape[0]
        own_count = count
        embed = every.shape[1]
        mix_gain[...] = depth_ref[...] * gain_ref[...]
        unit = summary_ref[:, width : width + embed]
        magnitude = summary_ref[:, width + embed : width + embed + 1]
        contract = (((1,), (1,)), ((), ()))
        gram = lax.dot_general(every, every, contract, preferred_element_type=F32)
        row_of = lax.broadcasted_iota(jnp.int32, (total_count, 1), 0)
        row_goal = lax.rem(row_of, own_count) < goal_total
        expon = jnp.where(row_goal, 0.0, jnp.exp(logit_scale * gram))
        column_total = jnp.sum(expon, axis=0, keepdims=True)
        scores = logit_scale * lax.dot_general(
            unit.astype(BF16), every, contract, preferred_element_type=F32
        )
        own_expon = jnp.exp(scores)
        column_of = lax.broadcasted_iota(jnp.int32, (own_count, total_count), 1)
        column_goal = lax.rem(column_of, own_count) < goal_total
        own_goal = lax.broadcasted_iota(jnp.int32, (own_count, total_count), 0) < goal_total
        own_total = jnp.sum(
            jnp.where(column_goal, 0.0, own_expon), axis=1, keepdims=True
        )
        own_index = position * own_count + lax.broadcasted_iota(
            jnp.int32, (own_count, total_count), 0
        )
        targets = column_target_ref[...]
        own_target = jnp.sum(
            jnp.where(column_of == own_index, targets.astype(F32), 0.0), axis=1, keepdims=True
        ).astype(jnp.int32)
        hit_goal = column_of == own_target
        hit_premise = targets == own_index
        of_goal = own_expon / own_total - jnp.where(hit_goal, 1.0, 0.0)
        of_premise = own_expon / column_total - jnp.where(hit_premise, 1.0, 0.0)
        score_grad = jnp.where(
            own_goal,
            jnp.where(column_goal, 0.0, of_goal),
            jnp.where(column_goal, of_premise, 0.0),
        )
        score_grad = (score_grad / float(goal_total)).astype(BF16)
        chosen = jnp.sum(jnp.where(hit_goal, scores, 0.0), axis=1, keepdims=True)
        loss_ref[...] = jnp.broadcast_to(jnp.log(own_total) - chosen, loss_ref.shape)
        unit_grad = logit_scale * jnp.dot(score_grad, every, preferred_element_type=F32)
        along = jnp.sum(unit * unit_grad, axis=-1, keepdims=True)
        embed_grad = ((unit_grad - unit * along) / magnitude).astype(BF16)
        head_grad[...] = lax.dot_general(
            summary_ref[:, :width].astype(BF16),
            embed_grad,
            (((0,), (0,)), ((), ())),
            preferred_element_type=F32,
        ).astype(BF16)
        upstream[...] = lax.dot_general(
            embed_grad, head_ref[...], contract, preferred_element_type=F32
        )

    def grad_up(seq, carry):
        row = pl.ds(step * SEQS + seq, 1)
        above = upstream[row, :] / scalars[step * SEQS + seq].astype(F32)
        upstream[row, :] = above
        for start in tiles:
            at = pl.ds(start, TILE)
            act_grad[seq, at, :] = (slope_up_ref[seq, at, :].astype(F32) * above).astype(BF16)
        return carry

    lax.fori_loop(0, SEQS, grad_up, 0)
    flat = act_grad[...].reshape(SEQS * length, width)
    conv_grad[:, PAD : PAD + length, :] = lax.dot_general(
        flat, weight_ref[0], (((1,), (1,)), ((), ())), preferred_element_type=F32
    ).reshape(SEQS, length, width)
    over_tokens = (((0,), (0,)), ((), ()))
    point_up[...] += lax.dot_general(
        mixed_up_ref[...].reshape(SEQS * length, width),
        flat,
        over_tokens,
        preferred_element_type=F32,
    )

    def norm_up(seq, carry):
        above = upstream[pl.ds(step * SEQS + seq, 1), :]
        sums = [corr[tap] for tap in range(3)]
        for start in tiles:
            at = pl.ds(start, TILE)
            normed = normed_up_ref[seq, at, :].astype(F32)
            inverse = inverse_ref[seq, at, :][:, :1]
            scaled = 0.0
            for tap in range(3):
                part = conv_grad[seq, pl.ds(PAD + start + (1 - tap) * UPPER_DILATION, TILE), :]
                scaled = scaled + mix_gain[tap, 1:2, :] * part
                product = part * normed
                sums[tap] = sums[tap] + product[:8] + product[8:]
            mean = jnp.mean(scaled * normed, axis=-1, keepdims=True)
            below = jnp.where(inverse > 0.0, above, 0.0) + inverse * (scaled - normed * mean)
            act_grad[seq, at, :] = (below * slope_low_ref[seq, at, :].astype(F32)).astype(BF16)
        for tap in range(3):
            corr[tap] = sums[tap]
        return carry

    lax.fori_loop(0, SEQS, norm_up, 0)
    moments[...] += lax.dot_general(
        act_grad[...].reshape(SEQS * length, width),
        shifted_ref[...].reshape(SEQS * length, 3 * width),
        over_tokens,
        preferred_element_type=F32,
    )

    def emit(low_ref, up_ref):
        point, rows = 0.0, []
        for tap in range(3):
            part = moments[:, tap * width : (tap + 1) * width]
            rows.append(
                jnp.sum(part * weight_turned_ref[...].astype(F32), axis=0, keepdims=True)
            )
            point = point + mix_gain[tap, 0:1, :] * part
        rows += [jnp.sum(corr[tap], axis=0, keepdims=True) for tap in range(3)]
        rows.append(jnp.zeros((2, width), F32))
        small = jnp.concatenate(rows, axis=0)
        low = point.T.astype(BF16)
        up = point_up[...].astype(BF16)
        for part in range(width // LANES):
            lanes = slice(part * LANES, (part + 1) * LANES)
            low_ref[part * width : (part + 1) * width, :] = low[:, lanes]
            up_ref[part * width : (part + 1) * width, :] = up[:, lanes]
        base = width * width // LANES
        for part in range(head_grad.shape[1] // LANES):
            lanes = slice(part * LANES, (part + 1) * LANES)
            low_ref[base + part * width : base + (part + 1) * width, :] = head_grad[:, lanes]
        tail = [small[:, part * LANES : (part + 1) * LANES] for part in range(width // LANES)]
        up_ref[base : base + 32, :] = jnp.concatenate(tail, axis=0).astype(BF16)
        up_ref[base + 32 :, :] = jnp.zeros((up_ref.shape[0] - base - 32, LANES), BF16)

    @pl.when((step == last) & (core == 0))
    def _():
        emit(keep_ref, send_ref)

    @pl.when((step == last) & (core == 1))
    def _():
        emit(send_ref, keep_ref)


def spread_kernel(parts_ref, spread_ref):
    total = parts_ref[0].astype(F32)
    for peer in range(1, parts_ref.shape[0]):
        total = total + parts_ref[peer].astype(F32)
    total = total.astype(BF16)
    for peer in range(parts_ref.shape[0]):
        spread_ref[peer] = total


def unpack_kernel(
    scalars,
    mine_ref,
    other_ref,
    depth_ref,
    gain_ref,
    depth_out,
    gain_out,
    point_out,
    head_out,
):
    core = scalars[scalars.shape[0] - 1]
    width = gain_ref.shape[1]
    base = width * width // LANES

    def emit(low_ref, up_ref):
        for part in range(width // LANES):
            lanes = slice(part * LANES, (part + 1) * LANES)
            rows = slice(part * width, (part + 1) * width)
            point_out[0, :, lanes] = low_ref[rows, :].astype(F32)
            point_out[1, :, lanes] = up_ref[rows, :].astype(F32)
        for part in range(head_out.shape[1] // LANES):
            lanes = slice(part * LANES, (part + 1) * LANES)
            head_out[:, lanes] = low_ref[
                base + part * width : base + (part + 1) * width, :
            ].astype(F32)
        small = up_ref[base : base + 32, :].astype(F32)
        for part in range(width // LANES):
            lanes = slice(part * LANES, (part + 1) * LANES)
            rows = small[part * 8 : (part + 1) * 8, :]
            for block in range(2):
                total = 0.0
                for tap in range(3):
                    row = rows[block * 3 + tap : block * 3 + tap + 1, :]
                    depth_out[tap, block : block + 1, lanes] = (
                        row * gain_ref[block : block + 1, lanes]
                    )
                    total = total + row * depth_ref[tap, block : block + 1, lanes]
                gain_out[block : block + 1, lanes] = total

    @pl.when(core == 0)
    def _():
        emit(mine_ref, other_ref)

    @pl.when(core == 1)
    def _():
        emit(other_ref, mine_ref)


goal_total = 8


def whole(shape):
    return pl.BlockSpec(shape, lambda i, *_: (0,) * len(shape))


def chunk(length, width):
    return pl.BlockSpec((SEQS, length, width), lambda i, *_: (i, 0, 0))


def run_forward(scalars, goal_states, premise_states, depth, gains, weights, head_weight):
    goals, length, width = goal_states.shape[1:]
    premises = premise_states.shape[1]
    count = goals + premises
    embed = head_weight.shape[1]
    goal_steps = goals // SEQS
    tokens = lambda w, t: jax.ShapeDtypeStruct((count, length, w), t)
    summary = (count, width + embed + LANES)
    outs = [
        (tokens(3 * width, BF16), chunk(length, 3 * width)),
        (tokens(width, BF16), chunk(length, width)),
        (tokens(width, BF16), chunk(length, width)),
        (tokens(width, BF16), chunk(length, width)),
        (tokens(width, BF16), chunk(length, width)),
        (tokens(LANES, F32), chunk(length, LANES)),
        (jax.ShapeDtypeStruct(summary, F32), whole(summary)),
        (
            jax.ShapeDtypeStruct((N_NEG, count, embed), BF16),
            whole((N_NEG, count, embed)),
        ),
    ]
    return pl.pallas_call(
        forward_kernel,
        name="forward",
        out_shape=[o[0] for o in outs],
        grid_spec=pltpu.PrefetchScalarGridSpec(
            num_scalar_prefetch=1,
            grid=(count // SEQS,),
            in_specs=[
                pl.BlockSpec(
                    (1, SEQS, length, width),
                    lambda i, *_: (0, jnp.minimum(i, goal_steps - 1), 0, 0),
                ),
                pl.BlockSpec(
                    (1, SEQS, length, width),
                    lambda i, *_: (0, jnp.maximum(i - goal_steps, 0), 0, 0),
                ),
                whole(depth.shape),
                whole(gains.shape),
                whole(weights.shape),
                whole(head_weight.shape),
            ],
            out_specs=[o[1] for o in outs],
            scratch_shapes=[
                pltpu.VMEM((SEQS, length, width), BF16),
                pltpu.VMEM((SEQS, length + 2 * PAD, width), F32),
                pltpu.VMEM((SEQS, length, width), BF16),
                pltpu.VMEM((SEQS, length, width), F32),
                pltpu.VMEM((SEQS, length, width), F32),
                pltpu.VMEM(depth.shape, F32),
            ],
        ),
        compiler_params=pltpu.CompilerParams(
            dimension_semantics=("arbitrary",), vmem_limit_bytes=60 << 20
        ),
    )(scalars, goal_states, premise_states, depth, gains, weights, head_weight)


def run_backward(scalars, tables, residuals):
    count, length, width = residuals[1].shape
    embed = tables[0].shape[1]
    depth = tables[4]
    half = (N_NEG * N_REP // 2 * SLICE, LANES)
    outs = [
        jax.ShapeDtypeStruct((count, LANES), F32),
        jax.ShapeDtypeStruct(half, BF16),
        jax.ShapeDtypeStruct(half, BF16),
    ]
    specs = [whole(t.shape) for t in tables]
    specs[6] = pl.BlockSpec((1, width, width), lambda i, *_: (1, 0, 0))
    return pl.pallas_call(
        backward_kernel,
        name="backward",
        out_shape=outs,
        grid_spec=pltpu.PrefetchScalarGridSpec(
            num_scalar_prefetch=1,
            grid=(count // SEQS,),
            in_specs=specs + [chunk(length, r.shape[2]) for r in residuals],
            out_specs=[whole(o.shape) for o in outs],
            scratch_shapes=[
                pltpu.VMEM((count, width), F32),
                pltpu.VMEM((SEQS, length, width), BF16),
                pltpu.VMEM((SEQS, length + 2 * PAD, width), F32),
                pltpu.VMEM((3, 8, width), F32),
                pltpu.VMEM((width, width), F32),
                pltpu.VMEM((width, 3 * width), F32),
                pltpu.VMEM((width, embed), BF16),
                pltpu.VMEM(depth.shape, F32),
            ],
        ),
        compiler_params=pltpu.CompilerParams(
            dimension_semantics=("arbitrary",), vmem_limit_bytes=60 << 20
        ),
    )(scalars, *tables, *residuals)


def reduce_everywhere(scalars, keep, send, depth, gains, embed):
    peers = N_NEG * N_REP // 2
    axes = ("neg", "chip")
    swap = [(0, 1), (1, 0)]
    width = gains.shape[1]
    got = lax.ppermute(send, "core", swap)
    pair = (keep.astype(F32) + got.astype(F32)).astype(BF16)
    parts = lax.all_to_all(pair.reshape(peers, SLICE, LANES), axes, 0, 0)
    spread = pl.pallas_call(
        spread_kernel, name="spread", out_shape=jax.ShapeDtypeStruct(parts.shape, BF16)
    )(parts)
    mine = lax.all_to_all(spread, axes, 0, 0).reshape(peers * SLICE, LANES)
    other = lax.ppermute(mine, "core", swap)
    vmem = pl.BlockSpec(memory_space=pltpu.VMEM)
    return pl.pallas_call(
        unpack_kernel,
        name="unpack",
        in_specs=[pl.BlockSpec(memory_space=pltpu.SMEM)] + [vmem] * 4,
        out_specs=[vmem] * 4,
        out_shape=[
            jax.ShapeDtypeStruct(depth.shape, F32),
            jax.ShapeDtypeStruct(gains.shape, F32),
            jax.ShapeDtypeStruct((2, width, width), F32),
            jax.ShapeDtypeStruct((width, embed), F32),
        ],
    )(scalars, mine, other, depth, gains)


def local(
    goal_states,
    premise_states,
    goal_ids,
    premise_ids,
    positives,
    depthwise_kernels,
    block_norm_gains,
    pointwise_weights,
    head_weight,
):
    goals = goal_states.shape[1]
    premises = premise_states.shape[1]
    count = goals + premises
    position = lax.axis_index("neg")
    lengths = jnp.sum(
        (jnp.concatenate([goal_ids[0], premise_ids[0]], axis=0) != 0).astype(jnp.int32), axis=1
    )
    scalars = jnp.concatenate(
        [lengths, jnp.stack([position, lax.axis_index("core")]).astype(jnp.int32)]
    )
    depth = depthwise_kernels.transpose(1, 0, 2)
    outs = run_forward(
        scalars,
        goal_states,
        premise_states,
        depth,
        block_norm_gains,
        pointwise_weights,
        head_weight,
    )
    residuals, (summary, spread) = outs[:6], outs[6:]
    gathered = lax.all_to_all(spread, "neg", 0, 0).reshape(N_NEG * count, -1)
    slot = positives[0] // premises * count + goals + positives[0] % premises
    slot = jnp.concatenate(
        [
            slot.reshape(N_NEG, goals).astype(jnp.int32),
            jnp.full((N_NEG, premises), -1, jnp.int32),
        ],
        axis=1,
    )
    tables = (
        gathered,
        summary,
        slot.reshape(1, N_NEG * count),
        head_weight,
        depth,
        block_norm_gains,
        pointwise_weights,
        pointwise_weights[0].T,
    )
    loss, keep, send = run_backward(scalars, tables, residuals)
    depth_grad, gain_grad, point_grad, head_grad = reduce_everywhere(
        scalars, keep, send, depth, block_norm_gains, head_weight.shape[1]
    )
    return (
        loss[:goals, 0][None, :],
        depth_grad.transpose(1, 0, 2),
        gain_grad,
        point_grad,
        head_grad,
    )


def solution(mesh):
    split = Mesh(mesh.devices.reshape(N_NEG, N_REP // 2, 2), ("neg", "chip", "core"))
    group = ("chip", "core")
    placed = (
        P(group, "neg", None, None),
        P(group, "neg", None, None),
        P(group, "neg", None),
        P(group, "neg", None),
        P(group, None),
        P(),
        P(),
        P(),
        P(),
    )
    return jax.shard_map(
        local,
        mesh=split,
        in_specs=placed,
        out_specs=(P(group, "neg"), P(), P(), P(), P()),
        check_vma=False,
    )
```

```python
import functools

import jax
import jax.numpy as jnp
from jax import lax
from jax.experimental import pallas as pl
from jax.experimental.pallas import tpu as pltpu
from jax.sharding import Mesh
from jax.sharding import PartitionSpec as P

LOWER_DILATION = 4
UPPER_DILATION = 8
N_NEG = 16
N_REP = 8
LANES = 128
PAD = 8
TILE = 16
CHUNK = 512
PART = 64
SUB = 256
EDGE = 16
SLICE = 48
EPS = 1e-06
GELU_C = 0.7978845608028654
GELU_A = 0.044715
logit_scale = 20.0
F32 = jnp.float32
BF16 = jnp.bfloat16


def gelu_parts(x):
    square = x * x
    half = 0.5 + 0.5 * jnp.tanh(x * (GELU_C + (GELU_C * GELU_A) * square))
    value = x * half
    slope = half + value * (1.0 - half) * (
        2.0 * GELU_C + (6.0 * GELU_C * GELU_A) * square
    )
    return value, slope


def table_of(scalars, start, count, shape, axis):
    place = lax.broadcasted_iota(jnp.int32, shape, axis)
    table = jnp.zeros(shape, jnp.int32)
    for seq in range(count):
        table = jnp.where(lax.rem(place, count) == seq, scalars[start + seq], table)
    return table


def last_chunk(scalars, count):
    return (scalars[2 * count] + CHUNK - 1) // CHUNK - 1


def wide(column):
    return jnp.concatenate([column] * 4, axis=1)


def forward_kernel(
    scalars,
    goal_ref,
    premise_ref,
    depth_ref,
    gain_ref,
    weight_ref,
    head_ref,
    normed_low_ref,
    slope_low_ref,
    normed_up_ref,
    inverse_ref,
    mixed_up_ref,
    slope_up_ref,
    summary_ref,
    spread_ref,
    arrived,
    states,
    valid_rows,
    padded_low,
    padded_up,
    hidden,
    mixed,
    squares,
    pre_act,
    pooling,
    mix_gain,
    semaphores,
):
    step = pl.program_id(0)
    goals, premises = goal_ref.shape[1], premise_ref.shape[1]
    count = goals + premises
    length, width = arrived.shape[1:]
    last = last_chunk(scalars, count)
    row_of = lax.broadcasted_iota(jnp.int32, (PART, LANES), 0)
    ones = jnp.ones((width, LANES), BF16)

    @pl.when(step == 0)
    def _():
        for group in range(count // goals):
            source = goal_ref.at[0] if group == 0 else premise_ref.at[
                0, pl.ds((group - 1) * goals, goals)
            ]
            pltpu.make_async_copy(
                source, arrived.at[pl.ds(group * goals, goals)], semaphores.at[group]
            ).start()
        end = (last + 1) * CHUNK
        edge = jnp.zeros((EDGE, width), BF16)
        padded_low[:EDGE, :] = edge
        padded_up[:EDGE, :] = edge
        padded_up[pl.ds(pl.multiple_of(EDGE + end, EDGE), EDGE), :] = edge
        padded_low[pl.ds(pl.multiple_of(EDGE + end, EDGE), EDGE), :] = edge
        mix_gain[...] = (depth_ref[...] * gain_ref[...]).astype(BF16)
        summary_ref[...] = jnp.zeros_like(summary_ref)
        pooling[0] = table_of(scalars, 0, count, (count, 1), 0)
        pooling[1] = table_of(scalars, count, count, (count, 1), 0)

        def clear(at):
            at = pl.multiple_of(at, TILE)
            states[pl.ds(at, TILE), :] = jnp.zeros((TILE, width), BF16)
            valid_rows[pl.ds(at, TILE), :] = jnp.zeros((TILE, LANES), F32)

        def one_sequence(seq, carry):
            @pl.when(lax.rem(seq, goals) == 0)
            def _():
                pltpu.make_async_copy(
                    goal_ref.at[0],
                    arrived.at[pl.ds(seq, goals)],
                    semaphores.at[lax.div(seq, goals)],
                ).wait()

            used, offset = scalars[seq], scalars[count + seq]

            def part(index, carry):
                start = pl.multiple_of(index * PART, PART)
                at = pl.ds(pl.multiple_of(offset + start, TILE), PART)
                states[at, :] = arrived[seq, pl.ds(start, PART), :]
                valid_rows[at, :] = jnp.where(row_of < used - start, 1.0, 0.0)
                return carry

            parts = (used + PART - 1) // PART
            lax.fori_loop(0, parts, part, 0)
            clear(offset + parts * PART)
            return carry

        lax.fori_loop(0, count, one_sequence, 0)

        def clear_tail(tile, carry):
            clear(scalars[2 * count] + tile * TILE)
            return carry

        lax.fori_loop(0, (end - scalars[2 * count]) // TILE, clear_tail, 0)

    def staged(first, second):
        for block in range(0, CHUNK + SUB, SUB):
            if block < CHUNK:
                first(block)
            if block:
                second(block - SUB)

    def rows_of(block):
        return range(block, block + SUB, TILE)

    def window_of(padded, base, start):
        return padded[pl.ds(pl.multiple_of(base + start, TILE), TILE + 2 * EDGE), :]

    def inverse_of(base, block):
        mean = jnp.dot(
            squares[block : block + SUB, :], ones, preferred_element_type=F32
        ) * (1.0 / width)
        place = pl.ds(pl.multiple_of(base + block, TILE), SUB)
        return (lax.rsqrt(mean + EPS) * valid_rows[place, :]).astype(BF16)

    @pl.when(step <= last)
    def _():
        base = step * CHUNK

        def square(block):
            raw = states[pl.ds(pl.multiple_of(base + block, TILE), SUB), :]
            squares[block : block + SUB, :] = raw * raw

        def scale(block):
            inverse = wide(inverse_of(base, block))
            raw = states[pl.ds(pl.multiple_of(base + block, TILE), SUB), :]
            padded_low[pl.ds(pl.multiple_of(EDGE + base + block, EDGE), SUB), :] = raw * inverse

        staged(square, scale)

    @pl.when((step >= 1) & (step <= last + 1))
    def _():
        base = (step - 1) * CHUNK
        slot = lax.rem(step + 1, 2)

        def mix_low(block):
            for start in rows_of(block):
                window = window_of(padded_low, base, start)
                at = pl.ds(start, TILE)
                total = None
                for tap in range(3):
                    first = EDGE + (tap - 1) * LOWER_DILATION
                    values = window[first : first + TILE]
                    term = mix_gain[tap, 0:1, :] * values
                    total = term if total is None else total + term
                    if tap == 1:
                        normed_low_ref[at, :] = values
                mixed[at, :] = total
            at = pl.ds(block, SUB)
            pre_act[at, :] = jnp.dot(
                mixed[at, :], weight_ref[0], preferred_element_type=F32
            ).astype(BF16)

        def act_low(block):
            for start in rows_of(block):
                at = pl.ds(start, TILE)
                place = pl.ds(pl.multiple_of(base + start, TILE), TILE)
                value, slope = gelu_parts(pre_act[at, :])
                slope_low_ref[at, :] = slope
                out = states[place, :] + value
                hidden[slot, at, :] = out
                squares[at, :] = out * out
            at = pl.ds(block, SUB)
            inverse = inverse_of(base, block)
            inverse_ref[at, :] = inverse
            normed = hidden[slot, at, :] * wide(inverse)
            padded_up[pl.ds(pl.multiple_of(EDGE + base + block, EDGE), SUB), :] = normed
            normed_up_ref[at, :] = normed

        staged(mix_low, act_low)

    @pl.when((step >= 2) & (step <= last + 2))
    def _():
        base = (step - 2) * CHUNK
        slot = lax.rem(step, 2)

        def mix_up(block):
            for start in rows_of(block):
                window = window_of(padded_up, base, start)
                total = None
                for tap in range(3):
                    first = EDGE + (tap - 1) * UPPER_DILATION
                    term = mix_gain[tap, 1:2, :] * window[first : first + TILE]
                    total = term if total is None else total + term
                mixed_up_ref[pl.ds(start, TILE), :] = total
            at = pl.ds(block, SUB)
            pre_act[at, :] = jnp.dot(
                mixed_up_ref[at, :], weight_ref[1], preferred_element_type=F32
            ).astype(BF16)

        def act_up(block):
            for start in rows_of(block):
                at = pl.ds(start, TILE)
                value, slope = gelu_parts(pre_act[at, :])
                slope_up_ref[at, :] = slope
                mixed[at, :] = hidden[slot, at, :] + value

        staged(mix_up, act_up)
        place = base + lax.broadcasted_iota(jnp.int32, (count, CHUNK), 1)
        begin = pooling[1]
        member = (place >= begin) & (place < begin + pooling[0])
        summary_ref[:, :width] += jnp.dot(
            jnp.where(member, 1.0, 0.0).astype(BF16), mixed[...], preferred_element_type=F32
        )

    @pl.when(step == pl.num_programs(0) - 1)
    def _():
        pooled = summary_ref[:, :width] / pooling[0].astype(F32)
        summary_ref[:, :width] = pooled
        embedded = jnp.dot(pooled.astype(BF16), head_ref[...], preferred_element_type=F32)
        magnitude = jnp.sqrt(jnp.sum(embedded * embedded, axis=-1, keepdims=True) + EPS)
        unit = embedded / magnitude
        embed = unit.shape[1]
        summary_ref[:, width : width + embed] = unit
        summary_ref[:, width + embed :] = jnp.broadcast_to(magnitude, (count, LANES))
        rounded = unit.astype(BF16)
        for peer in range(N_NEG):
            spread_ref[peer] = rounded


def backward_kernel(
    scalars,
    gathered_ref,
    summary_ref,
    column_target_ref,
    head_ref,
    depth_ref,
    gain_ref,
    weight_ref,
    weight_turned_ref,
    normed_low_ref,
    slope_low_ref,
    normed_up_ref,
    inverse_ref,
    mixed_up_ref,
    slope_up_ref,
    loss_ref,
    keep_ref,
    send_ref,
    pooled_grad,
    members,
    upstream,
    grad_up,
    grad_low,
    conv_grad,
    normed_low,
    shifted,
    scaled,
    products,
    corr,
    point_up,
    moments,
    head_grad,
    mix_gain,
    mix_half,
    semaphore,
):
    step = pl.program_id(0)
    last = pl.num_programs(0) - 1
    count = summary_ref.shape[0]
    position, core = scalars[2 * count + 1], scalars[2 * count + 2]
    width = grad_up.shape[1]
    rows = normed_low_ref.shape[0]
    final = last_chunk(scalars, count)

    after = pl.multiple_of(EDGE + (final + 1) * CHUNK, EDGE)

    def load_normed():
        return pltpu.make_async_copy(
            normed_low_ref, normed_low.at[pl.ds(EDGE, rows)], semaphore.at[0]
        )

    @pl.when(step == 0)
    def _():
        load_normed().start()
        zeros = jnp.zeros((EDGE, width), BF16)
        conv_grad[:EDGE, :] = zeros
        conv_grad[pl.ds(after, EDGE), :] = zeros
        mix_half[...] = (depth_ref[...] * gain_ref[...]).astype(BF16)
        members[0] = table_of(scalars, 0, count, (8, count), 1)
        members[1] = table_of(scalars, count, count, (8, count), 1)
        corr[...] = jnp.zeros_like(corr)
        point_up[...] = jnp.zeros_like(point_up)
        moments[...] = jnp.zeros_like(moments)
        every = gathered_ref[...]
        total_count = every.shape[0]
        own_count = count
        embed = every.shape[1]
        mix_gain[...] = depth_ref[...] * gain_ref[...]
        unit = summary_ref[:, width : width + embed]
        magnitude = summary_ref[:, width + embed : width + embed + 1]
        contract = (((1,), (1,)), ((), ()))
        gram = lax.dot_general(every, every, contract, preferred_element_type=F32)
        row_of = lax.broadcasted_iota(jnp.int32, (total_count, 1), 0)
        row_goal = lax.rem(row_of, own_count) < goal_total
        expon = jnp.where(row_goal, 0.0, jnp.exp(logit_scale * gram))
        column_total = jnp.sum(expon, axis=0, keepdims=True)
        scores = logit_scale * lax.dot_general(
            unit.astype(BF16), every, contract, preferred_element_type=F32
        )
        own_expon = jnp.exp(scores)
        column_of = lax.broadcasted_iota(jnp.int32, (own_count, total_count), 1)
        column_goal = lax.rem(column_of, own_count) < goal_total
        own_goal = lax.broadcasted_iota(jnp.int32, (own_count, total_count), 0) < goal_total
        own_total = jnp.sum(
            jnp.where(column_goal, 0.0, own_expon), axis=1, keepdims=True
        )
        own_index = position * own_count + lax.broadcasted_iota(
            jnp.int32, (own_count, total_count), 0
        )
        targets = column_target_ref[...]
        own_target = jnp.sum(
            jnp.where(column_of == own_index, targets.astype(F32), 0.0), axis=1, keepdims=True
        ).astype(jnp.int32)
        hit_goal = column_of == own_target
        hit_premise = targets == own_index
        of_goal = own_expon / own_total - jnp.where(hit_goal, 1.0, 0.0)
        of_premise = own_expon / column_total - jnp.where(hit_premise, 1.0, 0.0)
        score_grad = jnp.where(
            own_goal,
            jnp.where(column_goal, 0.0, of_goal),
            jnp.where(column_goal, of_premise, 0.0),
        )
        score_grad = (score_grad / float(goal_total)).astype(BF16)
        chosen = jnp.sum(jnp.where(hit_goal, scores, 0.0), axis=1, keepdims=True)
        loss_ref[...] = jnp.broadcast_to(jnp.log(own_total) - chosen, loss_ref.shape)
        unit_grad = logit_scale * jnp.dot(score_grad, every, preferred_element_type=F32)
        along = jnp.sum(unit * unit_grad, axis=-1, keepdims=True)
        embed_grad = ((unit_grad - unit * along) / magnitude).astype(BF16)
        head_grad[...] = lax.dot_general(
            summary_ref[:, :width].astype(BF16),
            embed_grad,
            (((0,), (0,)), ((), ())),
            preferred_element_type=F32,
        ).astype(BF16)
        used = table_of(scalars, 0, count, (count, 1), 0)
        spread_back = lax.dot_general(
            embed_grad, head_ref[...], contract, preferred_element_type=F32
        ) / used.astype(F32)
        pooled_grad[...] = spread_back.astype(BF16)

    over_tokens = (((0,), (0,)), ((), ()))
    blocks = range(0, CHUNK, SUB)

    @pl.when(step == 1)
    def _():
        load_normed().wait()
        zeros = jnp.zeros((EDGE, width), BF16)
        normed_low[:EDGE, :] = zeros
        normed_low[pl.ds(after, EDGE), :] = zeros

    @pl.when(step <= final)
    def _():
        base = step * CHUNK
        slot = lax.rem(step, 2)
        begin = members[1, 0:1, :]
        end = begin + members[0, 0:1, :]
        for block in blocks:
            at = pl.ds(block, SUB)
            place = base + block + lax.broadcasted_iota(jnp.int32, (SUB, count), 0)
            member = jnp.where((place >= begin) & (place < end), 1.0, 0.0).astype(BF16)
            above = jnp.dot(member, pooled_grad[...], preferred_element_type=F32).astype(BF16)
            upstream[slot, at, :] = above
            grad = slope_up_ref[at, :] * above
            grad_up[at, :] = grad
            conv_grad[pl.ds(pl.multiple_of(EDGE + base + block, EDGE), SUB), :] = (
                lax.dot_general(
                    grad, weight_ref[0], (((1,), (1,)), ((), ())), preferred_element_type=F32
                ).astype(BF16)
            )
        point_up[...] += lax.dot_general(
            mixed_up_ref[...], grad_up[...], over_tokens, preferred_element_type=F32
        )

    @pl.when((step >= 1) & (step <= final + 1))
    def _():
        base = (step - 1) * CHUNK
        slot = lax.rem(step + 1, 2)
        ones = jnp.ones((width, LANES), BF16)

        def mix(block):
            for start in range(block, block + SUB, TILE):
                at = pl.ds(start, TILE)
                place = pl.ds(pl.multiple_of(base + start, TILE), TILE + 2 * EDGE)
                window = conv_grad[place, :]
                states = normed_low[place, :]
                normed = normed_up_ref[at, :]
                total = None
                for tap in range(3):
                    first = EDGE + (1 - tap) * UPPER_DILATION
                    part = window[first : first + TILE]
                    term = mix_half[tap, 1:2, :] * part
                    total = term if total is None else total + term
                    products[tap, at, :] = part * normed
                    first = EDGE + (tap - 1) * LOWER_DILATION
                    shifted[at, tap * width : (tap + 1) * width] = states[first : first + TILE]
                scaled[at, :] = total
                products[3, at, :] = total * normed

        def back(block):
            at = pl.ds(block, SUB)
            mean = (
                jnp.dot(products[3, at, :], ones, preferred_element_type=F32) * (1.0 / width)
            ).astype(BF16)
            inner = scaled[at, :] - normed_up_ref[at, :] * wide(mean)
            below = upstream[slot, at, :] + wide(inverse_ref[at, :]) * inner
            grad_low[at, :] = below * slope_low_ref[at, :]

        for block in range(0, CHUNK + SUB, SUB):
            if block < CHUNK:
                mix(block)
            if block:
                back(block - SUB)
        every_row = jnp.ones((8, CHUNK), BF16)
        for tap in range(3):
            corr[tap] += jnp.dot(every_row, products[tap], preferred_element_type=F32)
        moments[...] += lax.dot_general(
            grad_low[...], shifted[...], over_tokens, preferred_element_type=F32
        )

    def emit(low_ref, up_ref):
        point, rows = 0.0, []
        for tap in range(3):
            part = moments[:, tap * width : (tap + 1) * width]
            rows.append(
                jnp.sum(part * weight_turned_ref[...].astype(F32), axis=0, keepdims=True)
            )
            point = point + mix_gain[tap, 0:1, :] * part
        rows += [corr[tap, 0:1, :] for tap in range(3)]
        rows.append(jnp.zeros((2, width), F32))
        small = jnp.concatenate(rows, axis=0)
        low = point.T.astype(BF16)
        up = point_up[...].astype(BF16)
        for part in range(width // LANES):
            lanes = slice(part * LANES, (part + 1) * LANES)
            low_ref[part * width : (part + 1) * width, :] = low[:, lanes]
            up_ref[part * width : (part + 1) * width, :] = up[:, lanes]
        base = width * width // LANES
        for part in range(head_grad.shape[1] // LANES):
            lanes = slice(part * LANES, (part + 1) * LANES)
            low_ref[base + part * width : base + (part + 1) * width, :] = head_grad[:, lanes]
        tail = [small[:, part * LANES : (part + 1) * LANES] for part in range(width // LANES)]
        up_ref[base : base + 32, :] = jnp.concatenate(tail, axis=0).astype(BF16)
        up_ref[base + 32 :, :] = jnp.zeros((up_ref.shape[0] - base - 32, LANES), BF16)

    @pl.when((step == last) & (core == 0))
    def _():
        emit(keep_ref, send_ref)

    @pl.when((step == last) & (core == 1))
    def _():
        emit(send_ref, keep_ref)


def spread_kernel(parts_ref, spread_ref):
    total = parts_ref[0].astype(F32)
    for peer in range(1, parts_ref.shape[0]):
        total = total + parts_ref[peer].astype(F32)
    total = total.astype(BF16)
    for peer in range(parts_ref.shape[0]):
        spread_ref[peer] = total


def unpack_kernel(
    scalars,
    mine_ref,
    other_ref,
    depth_ref,
    gain_ref,
    depth_out,
    gain_out,
    point_out,
    head_out,
):
    core = scalars[scalars.shape[0] - 1]
    width = gain_ref.shape[1]
    base = width * width // LANES

    def emit(low_ref, up_ref):
        for part in range(width // LANES):
            lanes = slice(part * LANES, (part + 1) * LANES)
            rows = slice(part * width, (part + 1) * width)
            point_out[0, :, lanes] = low_ref[rows, :].astype(F32)
            point_out[1, :, lanes] = up_ref[rows, :].astype(F32)
        for part in range(head_out.shape[1] // LANES):
            lanes = slice(part * LANES, (part + 1) * LANES)
            head_out[:, lanes] = low_ref[
                base + part * width : base + (part + 1) * width, :
            ].astype(F32)
        small = up_ref[base : base + 32, :].astype(F32)
        for part in range(width // LANES):
            lanes = slice(part * LANES, (part + 1) * LANES)
            rows = small[part * 8 : (part + 1) * 8, :]
            for block in range(2):
                total = 0.0
                for tap in range(3):
                    row = rows[block * 3 + tap : block * 3 + tap + 1, :]
                    depth_out[tap, block : block + 1, lanes] = (
                        row * gain_ref[block : block + 1, lanes]
                    )
                    total = total + row * depth_ref[tap, block : block + 1, lanes]
                gain_out[block : block + 1, lanes] = total

    @pl.when(core == 0)
    def _():
        emit(mine_ref, other_ref)

    @pl.when(core == 1)
    def _():
        emit(other_ref, mine_ref)


goal_total = 8


def whole(shape):
    return pl.BlockSpec(shape, lambda i, *_: (0,) * len(shape))


def run_forward(scalars, goal_states, premise_states, depth, gains, weights, head_weight):
    goals, length, width = goal_states.shape[1:]
    premises = premise_states.shape[1]
    count = goals + premises
    embed = head_weight.shape[1]
    chunks = -(-count * (length + TILE) // CHUNK)
    rows = chunks * CHUNK
    summary = (count, width + embed + LANES)

    def lower(columns):
        return pl.BlockSpec(
            (CHUNK, columns), lambda i, s: (jnp.clip(i - 1, 0, last_chunk(s, count)), 0)
        )

    upper = pl.BlockSpec(
        (CHUNK, width), lambda i, s: (jnp.clip(i - 2, 0, last_chunk(s, count)), 0)
    )
    packed = jax.ShapeDtypeStruct((rows, width), BF16)
    outs = [
        (packed, lower(width)),
        (packed, lower(width)),
        (packed, lower(width)),
        (jax.ShapeDtypeStruct((rows, LANES), BF16), lower(LANES)),
        (packed, upper),
        (packed, upper),
        (jax.ShapeDtypeStruct(summary, F32), whole(summary)),
        (
            jax.ShapeDtypeStruct((N_NEG, count, embed), BF16),
            whole((N_NEG, count, embed)),
        ),
    ]
    raw = pl.BlockSpec(memory_space=pl.ANY)
    return pl.pallas_call(
        forward_kernel,
        name="forward",
        out_shape=[o[0] for o in outs],
        grid_spec=pltpu.PrefetchScalarGridSpec(
            num_scalar_prefetch=1,
            grid=(chunks + 2,),
            in_specs=[
                raw,
                raw,
                whole(depth.shape),
                whole(gains.shape),
                whole(weights.shape),
                whole(head_weight.shape),
            ],
            out_specs=[o[1] for o in outs],
            scratch_shapes=[
                pltpu.VMEM((count, length, width), BF16),
                pltpu.VMEM((rows + PART + TILE, width), BF16),
                pltpu.VMEM((rows + PART + TILE, LANES), F32),
                pltpu.VMEM((rows + 2 * EDGE, width), BF16),
                pltpu.VMEM((rows + 2 * EDGE, width), BF16),
                pltpu.VMEM((2, CHUNK, width), BF16),
                pltpu.VMEM((CHUNK, width), BF16),
                pltpu.VMEM((CHUNK, width), BF16),
                pltpu.VMEM((CHUNK, width), BF16),
                pltpu.VMEM((2, count, 1), jnp.int32),
                pltpu.VMEM(depth.shape, BF16),
                pltpu.SemaphoreType.DMA((count // goals,)),
            ],
        ),
        compiler_params=pltpu.CompilerParams(
            dimension_semantics=("arbitrary",), vmem_limit_bytes=60 << 20
        ),
    )(scalars, goal_states, premise_states, depth, gains, weights, head_weight)


def run_backward(scalars, tables, residuals):
    rows, width = residuals[1].shape
    count = tables[1].shape[0]
    embed = tables[0].shape[1]
    depth = tables[4]
    half = (N_NEG * N_REP // 2 * SLICE, LANES)
    outs = [
        jax.ShapeDtypeStruct((count, LANES), F32),
        jax.ShapeDtypeStruct(half, BF16),
        jax.ShapeDtypeStruct(half, BF16),
    ]
    specs = [whole(t.shape) for t in tables]
    specs[6] = pl.BlockSpec((1, width, width), lambda i, *_: (1, 0, 0))

    def early(array):
        return pl.BlockSpec(
            (CHUNK, array.shape[1]), lambda i, s: (jnp.minimum(i, last_chunk(s, count)), 0)
        )

    def late(array):
        return pl.BlockSpec(
            (CHUNK, array.shape[1]),
            lambda i, s: (jnp.clip(i - 1, 0, last_chunk(s, count)), 0),
        )

    return pl.pallas_call(
        backward_kernel,
        name="backward",
        out_shape=outs,
        grid_spec=pltpu.PrefetchScalarGridSpec(
            num_scalar_prefetch=1,
            grid=(rows // CHUNK + 1,),
            in_specs=specs
            + [pl.BlockSpec(memory_space=pl.ANY)]
            + [late(r) for r in residuals[1:4]]
            + [early(r) for r in residuals[4:]],
            out_specs=[whole(o.shape) for o in outs],
            scratch_shapes=[
                pltpu.VMEM((count, width), BF16),
                pltpu.VMEM((2, 8, count), jnp.int32),
                pltpu.VMEM((2, CHUNK, width), BF16),
                pltpu.VMEM((CHUNK, width), BF16),
                pltpu.VMEM((CHUNK, width), BF16),
                pltpu.VMEM((rows + 2 * EDGE, width), BF16),
                pltpu.VMEM((rows + 2 * EDGE, width), BF16),
                pltpu.VMEM((CHUNK, 3 * width), BF16),
                pltpu.VMEM((CHUNK, width), BF16),
                pltpu.VMEM((4, CHUNK, width), BF16),
                pltpu.VMEM((3, 8, width), F32),
                pltpu.VMEM((width, width), F32),
                pltpu.VMEM((width, 3 * width), F32),
                pltpu.VMEM((width, embed), BF16),
                pltpu.VMEM(depth.shape, F32),
                pltpu.VMEM(depth.shape, BF16),
                pltpu.SemaphoreType.DMA((1,)),
            ],
        ),
        compiler_params=pltpu.CompilerParams(
            dimension_semantics=("arbitrary",), vmem_limit_bytes=60 << 20
        ),
    )(scalars, *tables, *residuals)


def reduce_everywhere(scalars, keep, send, depth, gains, embed):
    peers = N_NEG * N_REP // 2
    axes = ("neg", "chip")
    swap = [(0, 1), (1, 0)]
    width = gains.shape[1]
    got = lax.ppermute(send, "core", swap)
    pair = (keep.astype(F32) + got.astype(F32)).astype(BF16)
    parts = lax.all_to_all(pair.reshape(peers, SLICE, LANES), axes, 0, 0)
    spread = pl.pallas_call(
        spread_kernel, name="spread", out_shape=jax.ShapeDtypeStruct(parts.shape, BF16)
    )(parts)
    mine = lax.all_to_all(spread, axes, 0, 0).reshape(peers * SLICE, LANES)
    other = lax.ppermute(mine, "core", swap)
    vmem = pl.BlockSpec(memory_space=pltpu.VMEM)
    return pl.pallas_call(
        unpack_kernel,
        name="unpack",
        in_specs=[pl.BlockSpec(memory_space=pltpu.SMEM)] + [vmem] * 4,
        out_specs=[vmem] * 4,
        out_shape=[
            jax.ShapeDtypeStruct(depth.shape, F32),
            jax.ShapeDtypeStruct(gains.shape, F32),
            jax.ShapeDtypeStruct((2, width, width), F32),
            jax.ShapeDtypeStruct((width, embed), F32),
        ],
    )(scalars, mine, other, depth, gains)


def local(
    goal_states,
    premise_states,
    goal_ids,
    premise_ids,
    positives,
    depthwise_kernels,
    block_norm_gains,
    pointwise_weights,
    head_weight,
):
    goals = goal_states.shape[1]
    premises = premise_states.shape[1]
    count = goals + premises
    position = lax.axis_index("neg")
    lengths = jnp.sum(
        (jnp.concatenate([goal_ids[0], premise_ids[0]], axis=0) != 0).astype(jnp.int32), axis=1
    )
    room = (lengths + (PAD + TILE - 1)) // TILE * TILE
    places = jnp.arange(count + 1)
    starts = jnp.sum(
        jnp.where(places[None, :count] < places[:, None], room[None, :], 0), axis=1
    )
    scalars = jnp.concatenate(
        [lengths, starts, jnp.stack([position, lax.axis_index("core")])]
    ).astype(jnp.int32)
    depth = depthwise_kernels.transpose(1, 0, 2)
    outs = run_forward(
        scalars,
        goal_states,
        premise_states,
        depth,
        block_norm_gains,
        pointwise_weights,
        head_weight,
    )
    residuals, (summary, spread) = outs[:6], outs[6:]
    gathered = lax.all_to_all(spread, "neg", 0, 0).reshape(N_NEG * count, -1)
    slot = positives[0] // premises * count + goals + positives[0] % premises
    slot = jnp.concatenate(
        [
            slot.reshape(N_NEG, goals).astype(jnp.int32),
            jnp.full((N_NEG, premises), -1, jnp.int32),
        ],
        axis=1,
    )
    tables = (
        gathered,
        summary,
        slot.reshape(1, N_NEG * count),
        head_weight,
        depth,
        block_norm_gains,
        pointwise_weights,
        pointwise_weights[0].T,
    )
    loss, keep, send = run_backward(scalars, tables, residuals)
    depth_grad, gain_grad, point_grad, head_grad = reduce_everywhere(
        scalars, keep, send, depth, block_norm_gains, head_weight.shape[1]
    )
    return (
        loss[:goals, 0][None, :],
        depth_grad.transpose(1, 0, 2),
        gain_grad,
        point_grad,
        head_grad,
    )


def solution(mesh):
    split = Mesh(mesh.devices.reshape(N_NEG, N_REP // 2, 2), ("neg", "chip", "core"))
    group = ("chip", "core")
    placed = (
        P(group, "neg", None, None),
        P(group, "neg", None, None),
        P(group, "neg", None),
        P(group, "neg", None),
        P(group, None),
        P(),
        P(),
        P(),
        P(),
    )
    return jax.shard_map(
        local,
        mesh=split,
        in_specs=placed,
        out_specs=(P(group, "neg"), P(), P(), P(), P()),
        check_vma=False,
    )
```

```python
import functools

import jax
import jax.numpy as jnp
from jax import lax
from jax.experimental import pallas as pl
from jax.experimental.pallas import tpu as pltpu
from jax.sharding import Mesh
from jax.sharding import PartitionSpec as P

LOWER_DILATION = 4
UPPER_DILATION = 8
N_NEG = 16
N_REP = 8
LANES = 128
PAD = 8
TILE = 16
CHUNK = 512
PART = 64
SUB = 256
GROUP = 64
EDGE = 16
SLICE = 48
EPS = 1e-06
GELU_C = 0.7978845608028654
GELU_A = 0.044715
logit_scale = 20.0
F32 = jnp.float32
BF16 = jnp.bfloat16


def gelu_parts(x):
    square = x * x
    half = 0.5 + 0.5 * jnp.tanh(x * (GELU_C + (GELU_C * GELU_A) * square))
    value = x * half
    slope = half + value * (1.0 - half) * (
        2.0 * GELU_C + (6.0 * GELU_C * GELU_A) * square
    )
    return value, slope


def table_of(scalars, start, count, shape, axis):
    place = lax.broadcasted_iota(jnp.int32, shape, axis)
    table = jnp.zeros(shape, jnp.int32)
    for seq in range(count):
        table = jnp.where(lax.rem(place, count) == seq, scalars[start + seq], table)
    return table


def last_chunk(scalars, count):
    return (scalars[2 * count] + CHUNK - 1) // CHUNK - 1


def wide(column):
    return jnp.concatenate([column] * 4, axis=1)


def forward_kernel(
    scalars,
    goal_ref,
    premise_ref,
    depth_ref,
    gain_ref,
    weight_ref,
    head_ref,
    normed_low_ref,
    slope_low_ref,
    normed_up_ref,
    inverse_ref,
    mixed_up_ref,
    slope_up_ref,
    summary_ref,
    spread_ref,
    arrived,
    states,
    valid_rows,
    padded_low,
    padded_up,
    hidden,
    mixed,
    squares,
    pre_act,
    pooling,
    mix_gain,
    semaphores,
    next_sequence,
):
    step = pl.program_id(0)
    goals, premises = goal_ref.shape[1], premise_ref.shape[1]
    count = goals + premises
    length, width = arrived.shape[1:]
    last = last_chunk(scalars, count)
    row_of = lax.broadcasted_iota(jnp.int32, (PART, LANES), 0)
    ones = jnp.ones((width, LANES), BF16)

    @pl.when(step == 0)
    def _():
        for group in range(count // goals):
            source = goal_ref.at[0] if group == 0 else premise_ref.at[
                0, pl.ds((group - 1) * goals, goals)
            ]
            pltpu.make_async_copy(
                source, arrived.at[pl.ds(group * goals, goals)], semaphores.at[group]
            ).start()
        end = (last + 1) * CHUNK
        edge = jnp.zeros((EDGE, width), BF16)
        padded_low[:EDGE, :] = edge
        padded_up[:EDGE, :] = edge
        padded_up[pl.ds(pl.multiple_of(EDGE + end, EDGE), EDGE), :] = edge
        padded_low[pl.ds(pl.multiple_of(EDGE + end, EDGE), EDGE), :] = edge
        mix_gain[...] = (depth_ref[...] * gain_ref[...]).astype(BF16)
        summary_ref[...] = jnp.zeros_like(summary_ref)
        pooling[0] = table_of(scalars, 0, count, (count, 1), 0)
        pooling[1] = table_of(scalars, count, count, (count, 1), 0)
        next_sequence[0] = 0

    @pl.when(step <= last)
    def _():
        def clear(at):
            at = pl.multiple_of(at, TILE)
            states[pl.ds(at, TILE), :] = jnp.zeros((TILE, width), BF16)
            valid_rows[pl.ds(at, TILE), :] = jnp.zeros((TILE, LANES), F32)

        def wanted(seq):
            inside = jnp.minimum(seq, count - 1)
            return (seq < count) & (scalars[count + inside] < (step + 1) * CHUNK)

        def one_sequence(seq):
            @pl.when(lax.rem(seq, goals) == 0)
            def _():
                pltpu.make_async_copy(
                    goal_ref.at[0],
                    arrived.at[pl.ds(seq, goals)],
                    semaphores.at[lax.div(seq, goals)],
                ).wait()

            used, offset = scalars[seq], scalars[count + seq]

            def part(index, carry):
                start = pl.multiple_of(index * PART, PART)
                at = pl.ds(pl.multiple_of(offset + start, TILE), PART)
                states[at, :] = arrived[seq, pl.ds(start, PART), :]
                valid_rows[at, :] = jnp.where(row_of < used - start, 1.0, 0.0)
                return carry

            parts = (used + PART - 1) // PART
            lax.fori_loop(0, parts, part, 0)
            clear(offset + parts * PART)
            return seq + 1

        next_sequence[0] = lax.while_loop(wanted, one_sequence, next_sequence[0])

        @pl.when(step == last)
        def _():
            def clear_tail(tile, carry):
                clear(scalars[2 * count] + tile * TILE)
                return carry

            spare = (last + 1) * CHUNK - scalars[2 * count]
            lax.fori_loop(0, lax.div(spare, TILE), clear_tail, 0)

    def staged(first, second):
        for block in range(0, CHUNK + SUB, SUB):
            if block < CHUNK:
                first(block)
            if block:
                second(block - SUB)

    def rows_of(block):
        return range(block, block + SUB, TILE)

    def window_of(padded, base, start):
        return padded[pl.ds(pl.multiple_of(base + start, TILE), TILE + 2 * EDGE), :]

    def inverse_of(base, block):
        mean = jnp.dot(
            squares[block : block + SUB, :], ones, preferred_element_type=F32
        ) * (1.0 / width)
        place = pl.ds(pl.multiple_of(base + block, TILE), SUB)
        return (lax.rsqrt(mean + EPS) * valid_rows[place, :]).astype(BF16)

    @pl.when(step <= last)
    def _():
        base = step * CHUNK

        def square(block):
            raw = states[pl.ds(pl.multiple_of(base + block, TILE), SUB), :]
            squares[block : block + SUB, :] = raw * raw

        def scale(block):
            inverse = wide(inverse_of(base, block))
            raw = states[pl.ds(pl.multiple_of(base + block, TILE), SUB), :]
            padded_low[pl.ds(pl.multiple_of(EDGE + base + block, EDGE), SUB), :] = raw * inverse

        staged(square, scale)

    @pl.when((step >= 1) & (step <= last + 1))
    def _():
        base = (step - 1) * CHUNK
        slot = lax.rem(step + 1, 2)

        def mix_low(block):
            for start in rows_of(block):
                window = window_of(padded_low, base, start)
                at = pl.ds(start, TILE)
                total = None
                for tap in range(3):
                    first = EDGE + (tap - 1) * LOWER_DILATION
                    values = window[first : first + TILE]
                    term = mix_gain[tap, 0:1, :] * values
                    total = term if total is None else total + term
                    if tap == 1:
                        normed_low_ref[at, :] = values
                mixed[at, :] = total
            at = pl.ds(block, SUB)
            pre_act[at, :] = jnp.dot(
                mixed[at, :], weight_ref[0], preferred_element_type=F32
            ).astype(BF16)

        def act_low(block):
            for start in rows_of(block):
                at = pl.ds(start, TILE)
                place = pl.ds(pl.multiple_of(base + start, TILE), TILE)
                value, slope = gelu_parts(pre_act[at, :])
                slope_low_ref[at, :] = slope
                out = states[place, :] + value
                hidden[slot, at, :] = out
                squares[at, :] = out * out
            at = pl.ds(block, SUB)
            inverse = inverse_of(base, block)
            inverse_ref[at, :] = inverse
            normed = hidden[slot, at, :] * wide(inverse)
            padded_up[pl.ds(pl.multiple_of(EDGE + base + block, EDGE), SUB), :] = normed
            normed_up_ref[at, :] = normed

        staged(mix_low, act_low)

    @pl.when((step >= 2) & (step <= last + 2))
    def _():
        base = (step - 2) * CHUNK
        slot = lax.rem(step, 2)

        def mix_up(block):
            for start in rows_of(block):
                window = window_of(padded_up, base, start)
                total = None
                for tap in range(3):
                    first = EDGE + (tap - 1) * UPPER_DILATION
                    term = mix_gain[tap, 1:2, :] * window[first : first + TILE]
                    total = term if total is None else total + term
                mixed_up_ref[pl.ds(start, TILE), :] = total
            at = pl.ds(block, SUB)
            pre_act[at, :] = jnp.dot(
                mixed_up_ref[at, :], weight_ref[1], preferred_element_type=F32
            ).astype(BF16)

        def act_up(block):
            for start in rows_of(block):
                at = pl.ds(start, TILE)
                value, slope = gelu_parts(pre_act[at, :])
                slope_up_ref[at, :] = slope
                mixed[at, :] = hidden[slot, at, :] + value

        staged(mix_up, act_up)
        place = base + lax.broadcasted_iota(jnp.int32, (count, CHUNK), 1)
        begin = pooling[1]
        member = (place >= begin) & (place < begin + pooling[0])
        summary_ref[:, :width] += jnp.dot(
            jnp.where(member, 1.0, 0.0).astype(BF16), mixed[...], preferred_element_type=F32
        )

    @pl.when(step == pl.num_programs(0) - 1)
    def _():
        pooled = summary_ref[:, :width] / pooling[0].astype(F32)
        summary_ref[:, :width] = pooled
        embedded = jnp.dot(pooled.astype(BF16), head_ref[...], preferred_element_type=F32)
        magnitude = jnp.sqrt(jnp.sum(embedded * embedded, axis=-1, keepdims=True) + EPS)
        unit = embedded / magnitude
        embed = unit.shape[1]
        summary_ref[:, width : width + embed] = unit
        summary_ref[:, width + embed :] = jnp.broadcast_to(magnitude, (count, LANES))
        rounded = unit.astype(BF16)
        for peer in range(N_NEG):
            spread_ref[peer] = rounded


def backward_kernel(
    scalars,
    gathered_ref,
    summary_ref,
    column_target_ref,
    head_ref,
    depth_ref,
    gain_ref,
    weight_ref,
    normed_low_ref,
    slope_low_ref,
    normed_up_ref,
    inverse_ref,
    mixed_up_ref,
    slope_up_ref,
    loss_ref,
    keep_ref,
    send_ref,
    pooled_grad,
    members,
    upstream,
    grad_up,
    grad_low,
    conv_grad,
    normed_low,
    shifted,
    mixed_low,
    scaled,
    products,
    squares,
    corr,
    point_up,
    point_low,
    head_grad,
    mix_half,
    semaphore,
):
    step = pl.program_id(0)
    last = pl.num_programs(0) - 1
    count = summary_ref.shape[0]
    position, core = scalars[2 * count + 1], scalars[2 * count + 2]
    width = grad_up.shape[1]
    rows = normed_low_ref.shape[0]
    final = last_chunk(scalars, count)

    after = pl.multiple_of(EDGE + (final + 1) * CHUNK, EDGE)

    def load_normed():
        return pltpu.make_async_copy(
            normed_low_ref, normed_low.at[pl.ds(EDGE, rows)], semaphore.at[0]
        )

    @pl.when(step == 0)
    def _():
        load_normed().start()
        zeros = jnp.zeros((EDGE, width), BF16)
        conv_grad[:EDGE, :] = zeros
        conv_grad[pl.ds(after, EDGE), :] = zeros
        mix_half[...] = (depth_ref[...] * gain_ref[...]).astype(BF16)
        members[0] = table_of(scalars, 0, count, (8, count), 1)
        members[1] = table_of(scalars, count, count, (8, count), 1)
        corr[...] = jnp.zeros_like(corr)
        point_up[...] = jnp.zeros_like(point_up)
        point_low[...] = jnp.zeros_like(point_low)
        every = gathered_ref[...]
        total_count = every.shape[0]
        own_count = count
        embed = every.shape[1]
        unit = summary_ref[:, width : width + embed]
        magnitude = summary_ref[:, width + embed : width + embed + 1]
        contract = (((1,), (1,)), ((), ()))
        gram = lax.dot_general(every, every, contract, preferred_element_type=F32)
        row_of = lax.broadcasted_iota(jnp.int32, (total_count, 1), 0)
        row_goal = lax.rem(row_of, own_count) < goal_total
        expon = jnp.where(row_goal, 0.0, jnp.exp(logit_scale * gram))
        column_total = jnp.sum(expon, axis=0, keepdims=True)
        scores = logit_scale * lax.dot_general(
            unit.astype(BF16), every, contract, preferred_element_type=F32
        )
        own_expon = jnp.exp(scores)
        column_of = lax.broadcasted_iota(jnp.int32, (own_count, total_count), 1)
        column_goal = lax.rem(column_of, own_count) < goal_total
        own_goal = lax.broadcasted_iota(jnp.int32, (own_count, total_count), 0) < goal_total
        own_total = jnp.sum(
            jnp.where(column_goal, 0.0, own_expon), axis=1, keepdims=True
        )
        own_index = position * own_count + lax.broadcasted_iota(
            jnp.int32, (own_count, total_count), 0
        )
        targets = column_target_ref[...]
        own_target = jnp.sum(
            jnp.where(column_of == own_index, targets.astype(F32), 0.0), axis=1, keepdims=True
        ).astype(jnp.int32)
        hit_goal = column_of == own_target
        hit_premise = targets == own_index
        of_goal = own_expon / own_total - jnp.where(hit_goal, 1.0, 0.0)
        of_premise = own_expon / column_total - jnp.where(hit_premise, 1.0, 0.0)
        score_grad = jnp.where(
            own_goal,
            jnp.where(column_goal, 0.0, of_goal),
            jnp.where(column_goal, of_premise, 0.0),
        )
        score_grad = (score_grad / float(goal_total)).astype(BF16)
        chosen = jnp.sum(jnp.where(hit_goal, scores, 0.0), axis=1, keepdims=True)
        loss_ref[...] = jnp.broadcast_to(jnp.log(own_total) - chosen, loss_ref.shape)
        unit_grad = logit_scale * jnp.dot(score_grad, every, preferred_element_type=F32)
        along = jnp.sum(unit * unit_grad, axis=-1, keepdims=True)
        embed_grad = ((unit_grad - unit * along) / magnitude).astype(BF16)
        head_grad[...] = lax.dot_general(
            summary_ref[:, :width].astype(BF16),
            embed_grad,
            (((0,), (0,)), ((), ())),
            preferred_element_type=F32,
        ).astype(BF16)
        used = table_of(scalars, 0, count, (count, 1), 0)
        spread_back = lax.dot_general(
            embed_grad, head_ref[...], contract, preferred_element_type=F32
        ) / used.astype(F32)
        pooled_grad[...] = spread_back.astype(BF16)

    over_tokens = (((0,), (0,)), ((), ()))
    turned = (((1,), (1,)), ((), ()))
    blocks = range(0, CHUNK, SUB)

    @pl.when(step == 1)
    def _():
        load_normed().wait()
        zeros = jnp.zeros((EDGE, width), BF16)
        normed_low[:EDGE, :] = zeros
        normed_low[pl.ds(after, EDGE), :] = zeros

    @pl.when(step <= final)
    def _():
        base = step * CHUNK
        slot = lax.rem(step, 2)
        begin = members[1, 0:1, :]
        end = begin + members[0, 0:1, :]
        for block in blocks:
            at = pl.ds(block, SUB)
            place = base + block + lax.broadcasted_iota(jnp.int32, (SUB, count), 0)
            member = jnp.where((place >= begin) & (place < end), 1.0, 0.0).astype(BF16)
            above = jnp.dot(member, pooled_grad[...], preferred_element_type=F32).astype(BF16)
            upstream[slot, at, :] = above
            grad = slope_up_ref[at, :] * above
            grad_up[at, :] = grad
            conv_grad[pl.ds(pl.multiple_of(EDGE + base + block, EDGE), SUB), :] = (
                lax.dot_general(
                    grad, weight_ref[1], turned, preferred_element_type=F32
                ).astype(BF16)
            )
        point_up[...] += lax.dot_general(
            mixed_up_ref[...], grad_up[...], over_tokens, preferred_element_type=F32
        )

    @pl.when((step >= 1) & (step <= final + 1))
    def _():
        base = (step - 1) * CHUNK
        slot = lax.rem(step + 1, 2)
        ones = jnp.ones((width, LANES), BF16)

        def window_of(array, start):
            place = pl.ds(pl.multiple_of(base + start, TILE), TILE + 2 * EDGE)
            return array[place, :]

        def gather(sums, first, start, tap, product):
            sums[tap] = product if start % GROUP == 0 else sums[tap] + product
            if (start + TILE) % GROUP == 0:
                kept = start // GROUP * TILE
                products[first + tap, kept : kept + TILE, :] = sums[tap]

        def mix(block):
            sums = [None] * 3
            for start in range(block, block + SUB, TILE):
                at = pl.ds(start, TILE)
                window = window_of(conv_grad, start)
                states = window_of(normed_low, start)
                normed = normed_up_ref[at, :]
                total = low = None
                for tap in range(3):
                    first = EDGE + (1 - tap) * UPPER_DILATION
                    part = window[first : first + TILE]
                    term = mix_half[tap, 1:2, :] * part
                    total = term if total is None else total + term
                    gather(sums, 3, start, tap, part * normed)
                    first = EDGE + (tap - 1) * LOWER_DILATION
                    values = states[first : first + TILE]
                    shifted[tap, at, :] = values
                    term = mix_half[tap, 0:1, :] * values
                    low = term if low is None else low + term
                mixed_low[at, :] = low
                scaled[at, :] = total
                squares[at, :] = total * normed

        def back(block):
            at = pl.ds(block, SUB)
            mean = (
                jnp.dot(squares[at, :], ones, preferred_element_type=F32) * (1.0 / width)
            ).astype(BF16)
            inner = scaled[at, :] - normed_up_ref[at, :] * wide(mean)
            below = upstream[slot, at, :] + wide(inverse_ref[at, :]) * inner
            grad = below * slope_low_ref[at, :]
            grad_low[at, :] = grad
            scaled[at, :] = lax.dot_general(
                grad, weight_ref[0], turned, preferred_element_type=F32
            ).astype(BF16)

        def correlate(block):
            sums = [None] * 3
            for start in range(block, block + SUB, TILE):
                conv = scaled[start : start + TILE, :]
                for tap in range(3):
                    gather(sums, 0, start, tap, conv * shifted[tap, start : start + TILE, :])

        for block in range(0, CHUNK + 2 * SUB, SUB):
            if block < CHUNK:
                mix(block)
            if 0 <= block - SUB < CHUNK:
                back(block - SUB)
            if block >= 2 * SUB:
                correlate(block - 2 * SUB)
        every_row = jnp.ones((8, CHUNK // GROUP * TILE), BF16)
        for index in range(6):
            corr[index] += jnp.dot(every_row, products[index], preferred_element_type=F32)
        point_low[...] += lax.dot_general(
            mixed_low[...], grad_low[...], over_tokens, preferred_element_type=F32
        )

    def emit(low_ref, up_ref):
        rows = [corr[index, 0:1, :] for index in range(6)]
        rows.append(jnp.zeros((2, width), F32))
        small = jnp.concatenate(rows, axis=0)
        low = point_low[...].astype(BF16)
        up = point_up[...].astype(BF16)
        for part in range(width // LANES):
            lanes = slice(part * LANES, (part + 1) * LANES)
            low_ref[part * width : (part + 1) * width, :] = low[:, lanes]
            up_ref[part * width : (part + 1) * width, :] = up[:, lanes]
        base = width * width // LANES
        for part in range(head_grad.shape[1] // LANES):
            lanes = slice(part * LANES, (part + 1) * LANES)
            low_ref[base + part * width : base + (part + 1) * width, :] = head_grad[:, lanes]
        tail = [small[:, part * LANES : (part + 1) * LANES] for part in range(width // LANES)]
        up_ref[base : base + 32, :] = jnp.concatenate(tail, axis=0).astype(BF16)
        up_ref[base + 32 :, :] = jnp.zeros((up_ref.shape[0] - base - 32, LANES), BF16)

    @pl.when((step == last) & (core == 0))
    def _():
        emit(keep_ref, send_ref)

    @pl.when((step == last) & (core == 1))
    def _():
        emit(send_ref, keep_ref)


def spread_kernel(parts_ref, spread_ref):
    total = parts_ref[0].astype(F32)
    for peer in range(1, parts_ref.shape[0]):
        total = total + parts_ref[peer].astype(F32)
    total = total.astype(BF16)
    for peer in range(parts_ref.shape[0]):
        spread_ref[peer] = total


def unpack_kernel(
    scalars,
    mine_ref,
    other_ref,
    depth_ref,
    gain_ref,
    depth_out,
    gain_out,
    point_out,
    head_out,
):
    core = scalars[scalars.shape[0] - 1]
    width = gain_ref.shape[1]
    base = width * width // LANES

    def emit(low_ref, up_ref):
        for part in range(width // LANES):
            lanes = slice(part * LANES, (part + 1) * LANES)
            rows = slice(part * width, (part + 1) * width)
            point_out[0, :, lanes] = low_ref[rows, :].astype(F32)
            point_out[1, :, lanes] = up_ref[rows, :].astype(F32)
        for part in range(head_out.shape[1] // LANES):
            lanes = slice(part * LANES, (part + 1) * LANES)
            head_out[:, lanes] = low_ref[
                base + part * width : base + (part + 1) * width, :
            ].astype(F32)
        small = up_ref[base : base + 32, :].astype(F32)
        for part in range(width // LANES):
            lanes = slice(part * LANES, (part + 1) * LANES)
            rows = small[part * 8 : (part + 1) * 8, :]
            for block in range(2):
                total = 0.0
                for tap in range(3):
                    row = rows[block * 3 + tap : block * 3 + tap + 1, :]
                    depth_out[tap, block : block + 1, lanes] = (
                        row * gain_ref[block : block + 1, lanes]
                    )
                    total = total + row * depth_ref[tap, block : block + 1, lanes]
                gain_out[block : block + 1, lanes] = total

    @pl.when(core == 0)
    def _():
        emit(mine_ref, other_ref)

    @pl.when(core == 1)
    def _():
        emit(other_ref, mine_ref)


goal_total = 8


def whole(shape):
    return pl.BlockSpec(shape, lambda i, *_: (0,) * len(shape))


def run_forward(scalars, goal_states, premise_states, depth, gains, weights, head_weight):
    goals, length, width = goal_states.shape[1:]
    premises = premise_states.shape[1]
    count = goals + premises
    embed = head_weight.shape[1]
    chunks = -(-count * (length + TILE) // CHUNK)
    rows = chunks * CHUNK
    summary = (count, width + embed + LANES)

    def lower(columns):
        return pl.BlockSpec(
            (CHUNK, columns), lambda i, s: (jnp.clip(i - 1, 0, last_chunk(s, count)), 0)
        )

    upper = pl.BlockSpec(
        (CHUNK, width), lambda i, s: (jnp.clip(i - 2, 0, last_chunk(s, count)), 0)
    )
    packed = jax.ShapeDtypeStruct((rows, width), BF16)
    outs = [
        (packed, lower(width)),
        (packed, lower(width)),
        (packed, lower(width)),
        (jax.ShapeDtypeStruct((rows, LANES), BF16), lower(LANES)),
        (packed, upper),
        (packed, upper),
        (jax.ShapeDtypeStruct(summary, F32), whole(summary)),
        (
            jax.ShapeDtypeStruct((N_NEG, count, embed), BF16),
            whole((N_NEG, count, embed)),
        ),
    ]
    raw = pl.BlockSpec(memory_space=pl.ANY)
    return pl.pallas_call(
        forward_kernel,
        name="forward",
        out_shape=[o[0] for o in outs],
        grid_spec=pltpu.PrefetchScalarGridSpec(
            num_scalar_prefetch=1,
            grid=(chunks + 2,),
            in_specs=[
                raw,
                raw,
                whole(depth.shape),
                whole(gains.shape),
                whole(weights.shape),
                whole(head_weight.shape),
            ],
            out_specs=[o[1] for o in outs],
            scratch_shapes=[
                pltpu.VMEM((count, length, width), BF16),
                pltpu.VMEM((rows + PART + TILE, width), BF16),
                pltpu.VMEM((rows + PART + TILE, LANES), F32),
                pltpu.VMEM((rows + 2 * EDGE, width), BF16),
                pltpu.VMEM((rows + 2 * EDGE, width), BF16),
                pltpu.VMEM((2, CHUNK, width), BF16),
                pltpu.VMEM((CHUNK, width), BF16),
                pltpu.VMEM((CHUNK, width), BF16),
                pltpu.VMEM((CHUNK, width), BF16),
                pltpu.VMEM((2, count, 1), jnp.int32),
                pltpu.VMEM(depth.shape, BF16),
                pltpu.SemaphoreType.DMA((count // goals,)),
                pltpu.SMEM((1,), jnp.int32),
            ],
        ),
        compiler_params=pltpu.CompilerParams(
            dimension_semantics=("arbitrary",), vmem_limit_bytes=60 << 20
        ),
    )(scalars, goal_states, premise_states, depth, gains, weights, head_weight)


def run_backward(scalars, tables, residuals):
    rows, width = residuals[1].shape
    count = tables[1].shape[0]
    embed = tables[0].shape[1]
    depth = tables[4]
    half = (N_NEG * N_REP // 2 * SLICE, LANES)
    outs = [
        jax.ShapeDtypeStruct((count, LANES), F32),
        jax.ShapeDtypeStruct(half, BF16),
        jax.ShapeDtypeStruct(half, BF16),
    ]
    specs = [whole(t.shape) for t in tables]

    def early(array):
        return pl.BlockSpec(
            (CHUNK, array.shape[1]), lambda i, s: (jnp.minimum(i, last_chunk(s, count)), 0)
        )

    def late(array):
        return pl.BlockSpec(
            (CHUNK, array.shape[1]),
            lambda i, s: (jnp.clip(i - 1, 0, last_chunk(s, count)), 0),
        )

    return pl.pallas_call(
        backward_kernel,
        name="backward",
        out_shape=outs,
        grid_spec=pltpu.PrefetchScalarGridSpec(
            num_scalar_prefetch=1,
            grid=(rows // CHUNK + 1,),
            in_specs=specs
            + [pl.BlockSpec(memory_space=pl.ANY)]
            + [late(r) for r in residuals[1:4]]
            + [early(r) for r in residuals[4:]],
            out_specs=[whole(o.shape) for o in outs],
            scratch_shapes=[
                pltpu.VMEM((count, width), BF16),
                pltpu.VMEM((2, 8, count), jnp.int32),
                pltpu.VMEM((2, CHUNK, width), BF16),
                pltpu.VMEM((CHUNK, width), BF16),
                pltpu.VMEM((CHUNK, width), BF16),
                pltpu.VMEM((rows + 2 * EDGE, width), BF16),
                pltpu.VMEM((rows + 2 * EDGE, width), BF16),
                pltpu.VMEM((3, CHUNK, width), BF16),
                pltpu.VMEM((CHUNK, width), BF16),
                pltpu.VMEM((CHUNK, width), BF16),
                pltpu.VMEM((6, CHUNK // GROUP * TILE, width), BF16),
                pltpu.VMEM((CHUNK, width), BF16),
                pltpu.VMEM((6, 8, width), F32),
                pltpu.VMEM((width, width), F32),
                pltpu.VMEM((width, width), F32),
                pltpu.VMEM((width, embed), BF16),
                pltpu.VMEM(depth.shape, BF16),
                pltpu.SemaphoreType.DMA((1,)),
            ],
        ),
        compiler_params=pltpu.CompilerParams(
            dimension_semantics=("arbitrary",), vmem_limit_bytes=60 << 20
        ),
    )(scalars, *tables, *residuals)


def reduce_everywhere(scalars, keep, send, depth, gains, embed):
    peers = N_NEG * N_REP // 2
    axes = ("neg", "chip")
    swap = [(0, 1), (1, 0)]
    width = gains.shape[1]
    got = lax.ppermute(send, "core", swap)
    pair = (keep.astype(F32) + got.astype(F32)).astype(BF16)
    parts = lax.all_to_all(pair.reshape(peers, SLICE, LANES), axes, 0, 0)
    spread = pl.pallas_call(
        spread_kernel, name="spread", out_shape=jax.ShapeDtypeStruct(parts.shape, BF16)
    )(parts)
    mine = lax.all_to_all(spread, axes, 0, 0).reshape(peers * SLICE, LANES)
    other = lax.ppermute(mine, "core", swap)
    vmem = pl.BlockSpec(memory_space=pltpu.VMEM)
    return pl.pallas_call(
        unpack_kernel,
        name="unpack",
        in_specs=[pl.BlockSpec(memory_space=pltpu.SMEM)] + [vmem] * 4,
        out_specs=[vmem] * 4,
        out_shape=[
            jax.ShapeDtypeStruct(depth.shape, F32),
            jax.ShapeDtypeStruct(gains.shape, F32),
            jax.ShapeDtypeStruct((2, width, width), F32),
            jax.ShapeDtypeStruct((width, embed), F32),
        ],
    )(scalars, mine, other, depth, gains)


def local(
    goal_states,
    premise_states,
    goal_ids,
    premise_ids,
    positives,
    depthwise_kernels,
    block_norm_gains,
    pointwise_weights,
    head_weight,
):
    goals = goal_states.shape[1]
    premises = premise_states.shape[1]
    count = goals + premises
    position = lax.axis_index("neg")
    lengths = jnp.sum(
        (jnp.concatenate([goal_ids[0], premise_ids[0]], axis=0) != 0).astype(jnp.int32), axis=1
    )
    room = (lengths + (PAD + TILE - 1)) // TILE * TILE
    places = jnp.arange(count + 1)
    starts = jnp.sum(
        jnp.where(places[None, :count] < places[:, None], room[None, :], 0), axis=1
    )
    scalars = jnp.concatenate(
        [lengths, starts, jnp.stack([position, lax.axis_index("core")])]
    ).astype(jnp.int32)
    depth = depthwise_kernels.transpose(1, 0, 2)
    outs = run_forward(
        scalars,
        goal_states,
        premise_states,
        depth,
        block_norm_gains,
        pointwise_weights,
        head_weight,
    )
    residuals, (summary, spread) = outs[:6], outs[6:]
    gathered = lax.all_to_all(spread, "neg", 0, 0).reshape(N_NEG * count, -1)
    slot = positives[0] // premises * count + goals + positives[0] % premises
    slot = jnp.concatenate(
        [
            slot.reshape(N_NEG, goals).astype(jnp.int32),
            jnp.full((N_NEG, premises), -1, jnp.int32),
        ],
        axis=1,
    )
    tables = (
        gathered,
        summary,
        slot.reshape(1, N_NEG * count),
        head_weight,
        depth,
        block_norm_gains,
        pointwise_weights,
    )
    loss, keep, send = run_backward(scalars, tables, residuals)
    depth_grad, gain_grad, point_grad, head_grad = reduce_everywhere(
        scalars, keep, send, depth, block_norm_gains, head_weight.shape[1]
    )
    return (
        loss[:goals, 0][None, :],
        depth_grad.transpose(1, 0, 2),
        gain_grad,
        point_grad,
        head_grad,
    )


def solution(mesh):
    split = Mesh(mesh.devices.reshape(N_NEG, N_REP // 2, 2), ("neg", "chip", "core"))
    group = ("chip", "core")
    placed = (
        P(group, "neg", None, None),
        P(group, "neg", None, None),
        P(group, "neg", None),
        P(group, "neg", None),
        P(group, None),
        P(),
        P(),
        P(),
        P(),
    )
    return jax.shard_map(
        local,
        mesh=split,
        in_specs=placed,
        out_specs=(P(group, "neg"), P(), P(), P(), P()),
        check_vma=False,
    )
```

```python
import functools

import jax
import jax.numpy as jnp
from jax import lax
from jax.experimental import pallas as pl
from jax.experimental.pallas import tpu as pltpu
from jax.sharding import Mesh
from jax.sharding import PartitionSpec as P

LOWER_DILATION = 4
UPPER_DILATION = 8
N_NEG = 16
N_REP = 8
LANES = 128
PAD = 8
TILE = 16
CHUNK = 512
PART = 64
SUB = 256
GROUP = 64
EDGE = 16
SLICE = 48
EPS = 1e-06
GELU_C = 0.7978845608028654
GELU_A = 0.044715
logit_scale = 20.0
F32 = jnp.float32
BF16 = jnp.bfloat16


def gelu_parts(x):
    square = x * x
    half = 0.5 + 0.5 * jnp.tanh(x * (GELU_C + (GELU_C * GELU_A) * square))
    value = x * half
    slope = half + value * (1.0 - half) * (
        2.0 * GELU_C + (6.0 * GELU_C * GELU_A) * square
    )
    return value, slope


def table_of(scalars, start, count, shape, axis):
    place = lax.broadcasted_iota(jnp.int32, shape, axis)
    table = jnp.zeros(shape, jnp.int32)
    for seq in range(count):
        table = jnp.where(lax.rem(place, count) == seq, scalars[start + seq], table)
    return table


def last_chunk(scalars, count):
    return (scalars[2 * count] + CHUNK - 1) // CHUNK - 1


def wide(column):
    return jnp.concatenate([column] * 4, axis=1)


def forward_kernel(
    scalars,
    goal_ref,
    premise_ref,
    depth_ref,
    gain_ref,
    weight_ref,
    head_ref,
    normed_low_ref,
    slope_low_ref,
    normed_up_ref,
    inverse_ref,
    mixed_up_ref,
    slope_up_ref,
    summary_ref,
    spread_ref,
    arrived,
    states,
    valid_rows,
    padded_low,
    padded_up,
    hidden,
    mixed,
    squares,
    pre_act,
    pooling,
    mix_gain,
    semaphores,
    next_sequence,
):
    step = pl.program_id(0)
    goals, premises = goal_ref.shape[1], premise_ref.shape[1]
    count = goals + premises
    length, width = arrived.shape[1:]
    last = last_chunk(scalars, count)
    row_of = lax.broadcasted_iota(jnp.int32, (PART, LANES), 0)
    ones = jnp.ones((width, LANES), BF16)

    @pl.when(step == 0)
    def _():
        for group in range(count // goals):
            source = goal_ref.at[0] if group == 0 else premise_ref.at[
                0, pl.ds((group - 1) * goals, goals)
            ]
            pltpu.make_async_copy(
                source, arrived.at[pl.ds(group * goals, goals)], semaphores.at[group]
            ).start()
        end = (last + 1) * CHUNK
        edge = jnp.zeros((EDGE, width), BF16)
        padded_low[:EDGE, :] = edge
        padded_up[:EDGE, :] = edge
        padded_up[pl.ds(pl.multiple_of(EDGE + end, EDGE), EDGE), :] = edge
        padded_low[pl.ds(pl.multiple_of(EDGE + end, EDGE), EDGE), :] = edge
        mix_gain[...] = (depth_ref[...] * gain_ref[...]).astype(BF16)
        summary_ref[...] = jnp.zeros_like(summary_ref)
        pooling[0] = table_of(scalars, 0, count, (count, 1), 0)
        pooling[1] = table_of(scalars, count, count, (count, 1), 0)
        next_sequence[0] = 0

    @pl.when(step <= last)
    def _():
        def clear(at):
            at = pl.multiple_of(at, TILE)
            states[pl.ds(at, TILE), :] = jnp.zeros((TILE, width), BF16)
            valid_rows[pl.ds(at, TILE), :] = jnp.zeros((TILE, LANES), F32)

        def wanted(seq):
            inside = jnp.minimum(seq, count - 1)
            return (seq < count) & (scalars[count + inside] < (step + 1) * CHUNK)

        def one_sequence(seq):
            @pl.when(lax.rem(seq, goals) == 0)
            def _():
                pltpu.make_async_copy(
                    goal_ref.at[0],
                    arrived.at[pl.ds(seq, goals)],
                    semaphores.at[lax.div(seq, goals)],
                ).wait()

            used, offset = scalars[seq], scalars[count + seq]

            def part(index, carry):
                start = pl.multiple_of(index * PART, PART)
                at = pl.ds(pl.multiple_of(offset + start, TILE), PART)
                states[at, :] = arrived[seq, pl.ds(start, PART), :]
                valid_rows[at, :] = jnp.where(row_of < used - start, 1.0, 0.0)
                return carry

            parts = (used + PART - 1) // PART
            lax.fori_loop(0, parts, part, 0)
            clear(offset + parts * PART)
            return seq + 1

        next_sequence[0] = lax.while_loop(wanted, one_sequence, next_sequence[0])

        @pl.when(step == last)
        def _():
            def clear_tail(tile, carry):
                clear(scalars[2 * count] + tile * TILE)
                return carry

            spare = (last + 1) * CHUNK - scalars[2 * count]
            lax.fori_loop(0, lax.div(spare, TILE), clear_tail, 0)

    def staged(first, second):
        for block in range(0, CHUNK + SUB, SUB):
            if block < CHUNK:
                first(block)
            if block:
                second(block - SUB)

    def rows_of(block):
        return range(block, block + SUB, TILE)

    def window_of(padded, base, start):
        return padded[pl.ds(pl.multiple_of(base + start, TILE), TILE + 2 * EDGE), :]

    def inverse_of(base, block):
        mean = jnp.dot(
            squares[block : block + SUB, :], ones, preferred_element_type=F32
        ) * (1.0 / width)
        place = pl.ds(pl.multiple_of(base + block, TILE), SUB)
        return (lax.rsqrt(mean + EPS) * valid_rows[place, :]).astype(BF16)

    @pl.when(step <= last)
    def _():
        base = step * CHUNK

        def square(block):
            raw = states[pl.ds(pl.multiple_of(base + block, TILE), SUB), :]
            squares[block : block + SUB, :] = raw * raw

        def scale(block):
            inverse = wide(inverse_of(base, block))
            raw = states[pl.ds(pl.multiple_of(base + block, TILE), SUB), :]
            padded_low[pl.ds(pl.multiple_of(EDGE + base + block, EDGE), SUB), :] = raw * inverse

        staged(square, scale)

    @pl.when((step >= 1) & (step <= last + 1))
    def _():
        base = (step - 1) * CHUNK
        slot = lax.rem(step + 1, 2)

        def mix_low(block):
            for start in rows_of(block):
                window = window_of(padded_low, base, start)
                at = pl.ds(start, TILE)
                total = None
                for tap in range(3):
                    first = EDGE + (tap - 1) * LOWER_DILATION
                    values = window[first : first + TILE]
                    term = mix_gain[tap, 0:1, :] * values
                    total = term if total is None else total + term
                    if tap == 1:
                        normed_low_ref[at, :] = values
                mixed[at, :] = total
            at = pl.ds(block, SUB)
            pre_act[at, :] = jnp.dot(
                mixed[at, :], weight_ref[0], preferred_element_type=F32
            ).astype(BF16)

        def act_low(block):
            for start in rows_of(block):
                at = pl.ds(start, TILE)
                place = pl.ds(pl.multiple_of(base + start, TILE), TILE)
                value, slope = gelu_parts(pre_act[at, :])
                slope_low_ref[at, :] = slope
                out = states[place, :] + value
                hidden[slot, at, :] = out
                squares[at, :] = out * out
            at = pl.ds(block, SUB)
            inverse = inverse_of(base, block)
            inverse_ref[at, :] = inverse
            normed = hidden[slot, at, :] * wide(inverse)
            padded_up[pl.ds(pl.multiple_of(EDGE + base + block, EDGE), SUB), :] = normed
            normed_up_ref[at, :] = normed

        staged(mix_low, act_low)

    @pl.when((step >= 2) & (step <= last + 2))
    def _():
        base = (step - 2) * CHUNK
        slot = lax.rem(step, 2)

        def mix_up(block):
            for start in rows_of(block):
                window = window_of(padded_up, base, start)
                total = None
                for tap in range(3):
                    first = EDGE + (tap - 1) * UPPER_DILATION
                    term = mix_gain[tap, 1:2, :] * window[first : first + TILE]
                    total = term if total is None else total + term
                mixed_up_ref[pl.ds(start, TILE), :] = total
            at = pl.ds(block, SUB)
            pre_act[at, :] = jnp.dot(
                mixed_up_ref[at, :], weight_ref[1], preferred_element_type=F32
            ).astype(BF16)

        def act_up(block):
            for start in rows_of(block):
                at = pl.ds(start, TILE)
                value, slope = gelu_parts(pre_act[at, :])
                slope_up_ref[at, :] = slope
                mixed[at, :] = hidden[slot, at, :] + value

        staged(mix_up, act_up)
        place = base + lax.broadcasted_iota(jnp.int32, (count, CHUNK), 1)
        begin = pooling[1]
        member = (place >= begin) & (place < begin + pooling[0])
        summary_ref[:, :width] += jnp.dot(
            jnp.where(member, 1.0, 0.0).astype(BF16), mixed[...], preferred_element_type=F32
        )

    @pl.when(step == pl.num_programs(0) - 1)
    def _():
        pooled = summary_ref[:, :width] / pooling[0].astype(F32)
        summary_ref[:, :width] = pooled
        embedded = jnp.dot(pooled.astype(BF16), head_ref[...], preferred_element_type=F32)
        magnitude = jnp.sqrt(jnp.sum(embedded * embedded, axis=-1, keepdims=True) + EPS)
        unit = embedded / magnitude
        embed = unit.shape[1]
        summary_ref[:, width : width + embed] = unit
        summary_ref[:, width + embed :] = jnp.broadcast_to(magnitude, (count, LANES))
        rounded = unit.astype(BF16)
        for peer in range(N_NEG):
            spread_ref[peer] = rounded


def backward_kernel(
    scalars,
    gathered_ref,
    summary_ref,
    column_target_ref,
    head_ref,
    depth_ref,
    gain_ref,
    weight_ref,
    normed_low_ref,
    slope_low_ref,
    normed_up_ref,
    inverse_ref,
    mixed_up_ref,
    slope_up_ref,
    loss_ref,
    keep_ref,
    send_ref,
    pooled_grad,
    members,
    upstream,
    grad_up,
    grad_low,
    conv_grad,
    normed_low,
    shifted,
    mixed_low,
    scaled,
    products,
    squares,
    corr,
    point_up,
    point_low,
    head_grad,
    mix_half,
    semaphore,
):
    step = pl.program_id(0)
    last = pl.num_programs(0) - 1
    count = summary_ref.shape[0]
    position, core = scalars[2 * count + 1], scalars[2 * count + 2]
    width = grad_up.shape[1]
    rows = normed_low_ref.shape[0]
    final = last_chunk(scalars, count)

    after = pl.multiple_of(EDGE + (final + 1) * CHUNK, EDGE)

    def load_normed():
        return pltpu.make_async_copy(
            normed_low_ref, normed_low.at[pl.ds(EDGE, rows)], semaphore.at[0]
        )

    @pl.when(step == 0)
    def _():
        load_normed().start()
        zeros = jnp.zeros((EDGE, width), BF16)
        conv_grad[:EDGE, :] = zeros
        conv_grad[pl.ds(after, EDGE), :] = zeros
        mix_half[...] = (depth_ref[...] * gain_ref[...]).astype(BF16)
        members[0] = table_of(scalars, 0, count, (8, count), 1)
        members[1] = table_of(scalars, count, count, (8, count), 1)
        corr[...] = jnp.zeros_like(corr)
        point_up[...] = jnp.zeros_like(point_up)
        point_low[...] = jnp.zeros_like(point_low)
        every = gathered_ref[...]
        total_count = every.shape[0]
        own_count = count
        embed = every.shape[1]
        unit = summary_ref[:, width : width + embed]
        magnitude = summary_ref[:, width + embed : width + embed + 1]
        contract = (((1,), (1,)), ((), ()))
        gram = lax.dot_general(every, every, contract, preferred_element_type=F32)
        row_of = lax.broadcasted_iota(jnp.int32, (total_count, 1), 0)
        row_goal = lax.rem(row_of, own_count) < goal_total
        expon = jnp.where(row_goal, 0.0, jnp.exp(logit_scale * gram))
        column_total = jnp.sum(expon, axis=0, keepdims=True)
        scores = logit_scale * lax.dot_general(
            unit.astype(BF16), every, contract, preferred_element_type=F32
        )
        own_expon = jnp.exp(scores)
        column_of = lax.broadcasted_iota(jnp.int32, (own_count, total_count), 1)
        column_goal = lax.rem(column_of, own_count) < goal_total
        own_goal = lax.broadcasted_iota(jnp.int32, (own_count, total_count), 0) < goal_total
        own_total = jnp.sum(
            jnp.where(column_goal, 0.0, own_expon), axis=1, keepdims=True
        )
        own_index = position * own_count + lax.broadcasted_iota(
            jnp.int32, (own_count, total_count), 0
        )
        targets = column_target_ref[...]
        own_target = jnp.sum(
            jnp.where(column_of == own_index, targets.astype(F32), 0.0), axis=1, keepdims=True
        ).astype(jnp.int32)
        hit_goal = column_of == own_target
        hit_premise = targets == own_index
        of_goal = own_expon / own_total - jnp.where(hit_goal, 1.0, 0.0)
        of_premise = own_expon / column_total - jnp.where(hit_premise, 1.0, 0.0)
        score_grad = jnp.where(
            own_goal,
            jnp.where(column_goal, 0.0, of_goal),
            jnp.where(column_goal, of_premise, 0.0),
        )
        score_grad = (score_grad / float(goal_total)).astype(BF16)
        chosen = jnp.sum(jnp.where(hit_goal, scores, 0.0), axis=1, keepdims=True)
        lane = lax.broadcasted_iota(jnp.int32, (own_count, LANES), 1)
        diagonal = lane == lax.broadcasted_iota(jnp.int32, (own_count, LANES), 0)
        loss_ref[...] = jnp.sum(
            jnp.where(diagonal, jnp.log(own_total) - chosen, 0.0), axis=0, keepdims=True
        )
        unit_grad = logit_scale * jnp.dot(score_grad, every, preferred_element_type=F32)
        along = jnp.sum(unit * unit_grad, axis=-1, keepdims=True)
        embed_grad = ((unit_grad - unit * along) / magnitude).astype(BF16)
        head_grad[...] = lax.dot_general(
            summary_ref[:, :width].astype(BF16),
            embed_grad,
            (((0,), (0,)), ((), ())),
            preferred_element_type=F32,
        ).astype(BF16)
        used = table_of(scalars, 0, count, (count, 1), 0)
        spread_back = lax.dot_general(
            embed_grad, head_ref[...], contract, preferred_element_type=F32
        ) / used.astype(F32)
        pooled_grad[...] = spread_back.astype(BF16)

    over_tokens = (((0,), (0,)), ((), ()))
    turned = (((1,), (1,)), ((), ()))
    blocks = range(0, CHUNK, SUB)

    @pl.when(step == 1)
    def _():
        load_normed().wait()
        zeros = jnp.zeros((EDGE, width), BF16)
        normed_low[:EDGE, :] = zeros
        normed_low[pl.ds(after, EDGE), :] = zeros

    @pl.when(step <= final)
    def _():
        base = step * CHUNK
        slot = lax.rem(step, 2)
        begin = members[1, 0:1, :]
        end = begin + members[0, 0:1, :]
        for block in blocks:
            at = pl.ds(block, SUB)
            place = base + block + lax.broadcasted_iota(jnp.int32, (SUB, count), 0)
            member = jnp.where((place >= begin) & (place < end), 1.0, 0.0).astype(BF16)
            above = jnp.dot(member, pooled_grad[...], preferred_element_type=F32).astype(BF16)
            upstream[slot, at, :] = above
            grad = slope_up_ref[at, :] * above
            grad_up[at, :] = grad
            conv_grad[pl.ds(pl.multiple_of(EDGE + base + block, EDGE), SUB), :] = (
                lax.dot_general(
                    grad, weight_ref[1], turned, preferred_element_type=F32
                ).astype(BF16)
            )
        point_up[...] += lax.dot_general(
            mixed_up_ref[...], grad_up[...], over_tokens, preferred_element_type=F32
        )

    @pl.when((step >= 1) & (step <= final + 1))
    def _():
        base = (step - 1) * CHUNK
        slot = lax.rem(step + 1, 2)
        ones = jnp.ones((width, LANES), BF16)

        def window_of(array, start):
            place = pl.ds(pl.multiple_of(base + start, TILE), TILE + 2 * EDGE)
            return array[place, :]

        def gather(sums, first, start, tap, product):
            sums[tap] = product if start % GROUP == 0 else sums[tap] + product
            if (start + TILE) % GROUP == 0:
                kept = start // GROUP * TILE
                products[first + tap, kept : kept + TILE, :] = sums[tap]

        def mix(block):
            sums = [None] * 3
            for start in range(block, block + SUB, TILE):
                at = pl.ds(start, TILE)
                window = window_of(conv_grad, start)
                states = window_of(normed_low, start)
                normed = normed_up_ref[at, :]
                total = low = None
                for tap in range(3):
                    first = EDGE + (1 - tap) * UPPER_DILATION
                    part = window[first : first + TILE]
                    term = mix_half[tap, 1:2, :] * part
                    total = term if total is None else total + term
                    gather(sums, 3, start, tap, part * normed)
                    first = EDGE + (tap - 1) * LOWER_DILATION
                    values = states[first : first + TILE]
                    shifted[tap, at, :] = values
                    term = mix_half[tap, 0:1, :] * values
                    low = term if low is None else low + term
                mixed_low[at, :] = low
                scaled[at, :] = total
                squares[at, :] = total * normed

        def back(block):
            at = pl.ds(block, SUB)
            mean = (
                jnp.dot(squares[at, :], ones, preferred_element_type=F32) * (1.0 / width)
            ).astype(BF16)
            inner = scaled[at, :] - normed_up_ref[at, :] * wide(mean)
            below = upstream[slot, at, :] + wide(inverse_ref[at, :]) * inner
            grad = below * slope_low_ref[at, :]
            grad_low[at, :] = grad
            scaled[at, :] = lax.dot_general(
                grad, weight_ref[0], turned, preferred_element_type=F32
            ).astype(BF16)

        def correlate(block):
            sums = [None] * 3
            for start in range(block, block + SUB, TILE):
                conv = scaled[start : start + TILE, :]
                for tap in range(3):
                    gather(sums, 0, start, tap, conv * shifted[tap, start : start + TILE, :])

        for block in range(0, CHUNK + 2 * SUB, SUB):
            if block < CHUNK:
                mix(block)
            if 0 <= block - SUB < CHUNK:
                back(block - SUB)
            if block >= 2 * SUB:
                correlate(block - 2 * SUB)
        every_row = jnp.ones((8, CHUNK // GROUP * TILE), BF16)
        for index in range(6):
            corr[index] += jnp.dot(every_row, products[index], preferred_element_type=F32)
        point_low[...] += lax.dot_general(
            mixed_low[...], grad_low[...], over_tokens, preferred_element_type=F32
        )

    def emit(low_ref, up_ref):
        rows = [corr[index, 0:1, :] for index in range(6)]
        rows.append(jnp.zeros((2, width), F32))
        small = jnp.concatenate(rows, axis=0)
        low = point_low[...].astype(BF16)
        up = point_up[...].astype(BF16)
        for part in range(width // LANES):
            lanes = slice(part * LANES, (part + 1) * LANES)
            low_ref[part * width : (part + 1) * width, :] = low[:, lanes]
            up_ref[part * width : (part + 1) * width, :] = up[:, lanes]
        base = width * width // LANES
        for part in range(head_grad.shape[1] // LANES):
            lanes = slice(part * LANES, (part + 1) * LANES)
            low_ref[base + part * width : base + (part + 1) * width, :] = head_grad[:, lanes]
        tail = [small[:, part * LANES : (part + 1) * LANES] for part in range(width // LANES)]
        up_ref[base : base + 32, :] = jnp.concatenate(tail, axis=0).astype(BF16)
        up_ref[base + 32 :, :] = jnp.zeros((up_ref.shape[0] - base - 32, LANES), BF16)

    @pl.when((step == last) & (core == 0))
    def _():
        emit(keep_ref, send_ref)

    @pl.when((step == last) & (core == 1))
    def _():
        emit(send_ref, keep_ref)


def spread_kernel(parts_ref, spread_ref):
    total = parts_ref[0].astype(F32)
    for peer in range(1, parts_ref.shape[0]):
        total = total + parts_ref[peer].astype(F32)
    total = total.astype(BF16)
    for peer in range(parts_ref.shape[0]):
        spread_ref[peer] = total


def unpack_kernel(
    scalars,
    mine_ref,
    other_ref,
    depth_ref,
    gain_ref,
    depth_out,
    gain_out,
    point_out,
    head_out,
):
    core = scalars[scalars.shape[0] - 1]
    part = pl.program_id(0)
    width = point_out.shape[1]
    base = width * width // LANES

    def emit(low_ref, up_ref):
        rows = pl.ds(pl.multiple_of(part * width, width), width)
        point_out[0] = low_ref[rows, :].astype(F32)
        point_out[1] = up_ref[rows, :].astype(F32)

        @pl.when(part < 2)
        def _():
            head_rows = pl.ds(pl.multiple_of(base + part * width, width), width)
            head_out[...] = low_ref[head_rows, :].astype(F32)

        small = up_ref[base : base + 32, :].astype(F32)
        chosen = small[:8]
        for other in range(1, width // LANES):
            chosen = jnp.where(part == other, small[other * 8 : other * 8 + 8], chosen)
        for block in range(2):
            total = 0.0
            for tap in range(3):
                row = chosen[block * 3 + tap : block * 3 + tap + 1, :]
                depth_out[tap, block : block + 1, :] = row * gain_ref[block : block + 1, :]
                total = total + row * depth_ref[tap, block : block + 1, :]
            gain_out[block : block + 1, :] = total

    @pl.when(core == 0)
    def _():
        emit(mine_ref, other_ref)

    @pl.when(core == 1)
    def _():
        emit(other_ref, mine_ref)


goal_total = 8


def whole(shape):
    return pl.BlockSpec(shape, lambda i, *_: (0,) * len(shape))


def run_forward(scalars, goal_states, premise_states, depth, gains, weights, head_weight):
    goals, length, width = goal_states.shape[1:]
    premises = premise_states.shape[1]
    count = goals + premises
    embed = head_weight.shape[1]
    chunks = -(-count * (length + TILE) // CHUNK)
    rows = chunks * CHUNK
    summary = (count, width + embed + LANES)

    def lower(columns):
        return pl.BlockSpec(
            (CHUNK, columns), lambda i, s: (jnp.clip(i - 1, 0, last_chunk(s, count)), 0)
        )

    upper = pl.BlockSpec(
        (CHUNK, width), lambda i, s: (jnp.clip(i - 2, 0, last_chunk(s, count)), 0)
    )
    packed = jax.ShapeDtypeStruct((rows, width), BF16)
    outs = [
        (packed, lower(width)),
        (packed, lower(width)),
        (packed, lower(width)),
        (jax.ShapeDtypeStruct((rows, LANES), BF16), lower(LANES)),
        (packed, upper),
        (packed, upper),
        (jax.ShapeDtypeStruct(summary, F32), whole(summary)),
        (
            jax.ShapeDtypeStruct((N_NEG, count, embed), BF16),
            whole((N_NEG, count, embed)),
        ),
    ]
    raw = pl.BlockSpec(memory_space=pl.ANY)
    return pl.pallas_call(
        forward_kernel,
        name="forward",
        out_shape=[o[0] for o in outs],
        grid_spec=pltpu.PrefetchScalarGridSpec(
            num_scalar_prefetch=1,
            grid=(chunks + 2,),
            in_specs=[
                raw,
                raw,
                whole(depth.shape),
                whole(gains.shape),
                whole(weights.shape),
                whole(head_weight.shape),
            ],
            out_specs=[o[1] for o in outs],
            scratch_shapes=[
                pltpu.VMEM((count, length, width), BF16),
                pltpu.VMEM((rows + PART + TILE, width), BF16),
                pltpu.VMEM((rows + PART + TILE, LANES), F32),
                pltpu.VMEM((rows + 2 * EDGE, width), BF16),
                pltpu.VMEM((rows + 2 * EDGE, width), BF16),
                pltpu.VMEM((2, CHUNK, width), BF16),
                pltpu.VMEM((CHUNK, width), BF16),
                pltpu.VMEM((CHUNK, width), BF16),
                pltpu.VMEM((CHUNK, width), BF16),
                pltpu.VMEM((2, count, 1), jnp.int32),
                pltpu.VMEM(depth.shape, BF16),
                pltpu.SemaphoreType.DMA((count // goals,)),
                pltpu.SMEM((1,), jnp.int32),
            ],
        ),
        compiler_params=pltpu.CompilerParams(
            dimension_semantics=("arbitrary",), vmem_limit_bytes=60 << 20
        ),
    )(scalars, goal_states, premise_states, depth, gains, weights, head_weight)


def run_backward(scalars, tables, residuals):
    rows, width = residuals[1].shape
    count = tables[1].shape[0]
    embed = tables[0].shape[1]
    depth = tables[4]
    half = (N_NEG * N_REP // 2 * SLICE, LANES)
    outs = [
        jax.ShapeDtypeStruct((1, LANES), F32),
        jax.ShapeDtypeStruct(half, BF16),
        jax.ShapeDtypeStruct(half, BF16),
    ]
    specs = [whole(t.shape) for t in tables]

    def early(array):
        return pl.BlockSpec(
            (CHUNK, array.shape[1]), lambda i, s: (jnp.minimum(i, last_chunk(s, count)), 0)
        )

    def late(array):
        return pl.BlockSpec(
            (CHUNK, array.shape[1]),
            lambda i, s: (jnp.clip(i - 1, 0, last_chunk(s, count)), 0),
        )

    return pl.pallas_call(
        backward_kernel,
        name="backward",
        out_shape=outs,
        grid_spec=pltpu.PrefetchScalarGridSpec(
            num_scalar_prefetch=1,
            grid=(rows // CHUNK + 1,),
            in_specs=specs
            + [pl.BlockSpec(memory_space=pl.ANY)]
            + [late(r) for r in residuals[1:4]]
            + [early(r) for r in residuals[4:]],
            out_specs=[whole(o.shape) for o in outs],
            scratch_shapes=[
                pltpu.VMEM((count, width), BF16),
                pltpu.VMEM((2, 8, count), jnp.int32),
                pltpu.VMEM((2, CHUNK, width), BF16),
                pltpu.VMEM((CHUNK, width), BF16),
                pltpu.VMEM((CHUNK, width), BF16),
                pltpu.VMEM((rows + 2 * EDGE, width), BF16),
                pltpu.VMEM((rows + 2 * EDGE, width), BF16),
                pltpu.VMEM((3, CHUNK, width), BF16),
                pltpu.VMEM((CHUNK, width), BF16),
                pltpu.VMEM((CHUNK, width), BF16),
                pltpu.VMEM((6, CHUNK // GROUP * TILE, width), BF16),
                pltpu.VMEM((CHUNK, width), BF16),
                pltpu.VMEM((6, 8, width), F32),
                pltpu.VMEM((width, width), F32),
                pltpu.VMEM((width, width), F32),
                pltpu.VMEM((width, embed), BF16),
                pltpu.VMEM(depth.shape, BF16),
                pltpu.SemaphoreType.DMA((1,)),
            ],
        ),
        compiler_params=pltpu.CompilerParams(
            dimension_semantics=("arbitrary",), vmem_limit_bytes=60 << 20
        ),
    )(scalars, *tables, *residuals)


def reduce_everywhere(scalars, keep, send, depth, gains, embed):
    peers = N_NEG * N_REP // 2
    axes = ("neg", "chip")
    swap = [(0, 1), (1, 0)]
    width = gains.shape[1]
    got = lax.ppermute(send, "core", swap)
    pair = (keep.astype(F32) + got.astype(F32)).astype(BF16)
    parts = lax.all_to_all(pair.reshape(peers, SLICE, LANES), axes, 0, 0)
    spread = pl.pallas_call(
        spread_kernel, name="spread", out_shape=jax.ShapeDtypeStruct(parts.shape, BF16)
    )(parts)
    mine = lax.all_to_all(spread, axes, 0, 0).reshape(peers * SLICE, LANES)
    other = lax.ppermute(mine, "core", swap)
    vmem = pl.BlockSpec(memory_space=pltpu.VMEM)
    return pl.pallas_call(
        unpack_kernel,
        name="unpack",
        grid=(width // LANES,),
        in_specs=[
            pl.BlockSpec(memory_space=pltpu.SMEM),
            vmem,
            vmem,
            pl.BlockSpec((3, 2, LANES), lambda i: (0, 0, i)),
            pl.BlockSpec((2, LANES), lambda i: (0, i)),
        ],
        out_specs=[
            pl.BlockSpec((3, 2, LANES), lambda i: (0, 0, i)),
            pl.BlockSpec((2, LANES), lambda i: (0, i)),
            pl.BlockSpec((2, width, LANES), lambda i: (0, 0, i)),
            pl.BlockSpec((width, LANES), lambda i: (0, jnp.minimum(i, 1))),
        ],
        out_shape=[
            jax.ShapeDtypeStruct(depth.shape, F32),
            jax.ShapeDtypeStruct(gains.shape, F32),
            jax.ShapeDtypeStruct((2, width, width), F32),
            jax.ShapeDtypeStruct((width, embed), F32),
        ],
    )(scalars, mine, other, depth, gains)


def local(
    goal_states,
    premise_states,
    goal_ids,
    premise_ids,
    positives,
    depthwise_kernels,
    block_norm_gains,
    pointwise_weights,
    head_weight,
):
    goals = goal_states.shape[1]
    premises = premise_states.shape[1]
    count = goals + premises
    position = lax.axis_index("neg")
    lengths = jnp.sum(
        (jnp.concatenate([goal_ids[0], premise_ids[0]], axis=0) != 0).astype(jnp.int32), axis=1
    )
    room = (lengths + (PAD + TILE - 1)) // TILE * TILE
    places = jnp.arange(count + 1)
    starts = jnp.sum(
        jnp.where(places[None, :count] < places[:, None], room[None, :], 0), axis=1
    )
    scalars = jnp.concatenate(
        [lengths, starts, jnp.stack([position, lax.axis_index("core")])]
    ).astype(jnp.int32)
    depth = depthwise_kernels.transpose(1, 0, 2)
    outs = run_forward(
        scalars,
        goal_states,
        premise_states,
        depth,
        block_norm_gains,
        pointwise_weights,
        head_weight,
    )
    residuals, (summary, spread) = outs[:6], outs[6:]
    gathered = lax.all_to_all(spread, "neg", 0, 0).reshape(N_NEG * count, -1)
    slot = positives[0] // premises * count + goals + positives[0] % premises
    slot = jnp.concatenate(
        [
            slot.reshape(N_NEG, goals).astype(jnp.int32),
            jnp.full((N_NEG, premises), -1, jnp.int32),
        ],
        axis=1,
    )
    tables = (
        gathered,
        summary,
        slot.reshape(1, N_NEG * count),
        head_weight,
        depth,
        block_norm_gains,
        pointwise_weights,
    )
    loss, keep, send = run_backward(scalars, tables, residuals)
    depth_grad, gain_grad, point_grad, head_grad = reduce_everywhere(
        scalars, keep, send, depth, block_norm_gains, head_weight.shape[1]
    )
    return (
        loss[:, :goals],
        depth_grad.transpose(1, 0, 2),
        gain_grad,
        point_grad,
        head_grad,
    )


def solution(mesh):
    split = Mesh(mesh.devices.reshape(N_NEG, N_REP // 2, 2), ("neg", "chip", "core"))
    group = ("chip", "core")
    placed = (
        P(group, "neg", None, None),
        P(group, "neg", None, None),
        P(group, "neg", None),
        P(group, "neg", None),
        P(group, None),
        P(),
        P(),
        P(),
        P(),
    )
    return jax.shard_map(
        local,
        mesh=split,
        in_specs=placed,
        out_specs=(P(group, "neg"), P(), P(), P(), P()),
        check_vma=False,
    )
```

```python
import functools

import jax
import jax.numpy as jnp
from jax import lax
from jax.experimental import pallas as pl
from jax.experimental.pallas import tpu as pltpu
from jax.sharding import Mesh
from jax.sharding import PartitionSpec as P

LOWER_DILATION = 4
UPPER_DILATION = 8
N_NEG = 16
N_REP = 8
LANES = 128
PAD = 8
TILE = 16
CHUNK = 512
PART = 64
SUB = 256
GROUP = 64
EDGE = 16
SLICE = 48
EPS = 1e-06
GELU_C = 0.7978845608028654
GELU_A = 0.044715
logit_scale = 20.0
F32 = jnp.float32
BF16 = jnp.bfloat16


def gelu_parts(x):
    square = x * x
    half = 0.5 + 0.5 * jnp.tanh(x * (GELU_C + (GELU_C * GELU_A) * square))
    value = x * half
    slope = half + value * (1.0 - half) * (
        2.0 * GELU_C + (6.0 * GELU_C * GELU_A) * square
    )
    return value, slope


def table_of(scalars, start, count, shape, axis):
    place = lax.broadcasted_iota(jnp.int32, shape, axis)
    table = jnp.zeros(shape, jnp.int32)
    for seq in range(count):
        table = jnp.where(lax.rem(place, count) == seq, scalars[start + seq], table)
    return table


def last_chunk(scalars, count):
    return (scalars[2 * count] + CHUNK - 1) // CHUNK - 1


def wide(column):
    return jnp.concatenate([column] * 4, axis=1)


def forward_kernel(
    scalars,
    goal_ref,
    premise_ref,
    depth_ref,
    gain_ref,
    weight_ref,
    head_ref,
    normed_low_ref,
    slope_low_ref,
    normed_up_ref,
    inverse_ref,
    mixed_up_ref,
    slope_up_ref,
    summary_ref,
    spread_ref,
    arrived,
    states,
    valid_rows,
    padded_low,
    padded_up,
    hidden,
    mixed,
    squares,
    pre_act,
    pooling,
    mix_gain,
    semaphores,
    next_sequence,
):
    step = pl.program_id(0)
    goals, premises = goal_ref.shape[1], premise_ref.shape[1]
    count = goals + premises
    length, width = arrived.shape[1:]
    last = last_chunk(scalars, count)
    row_of = lax.broadcasted_iota(jnp.int32, (PART, LANES), 0)
    ones = jnp.ones((width, LANES), BF16)

    @pl.when(step == 0)
    def _():
        for group in range(count // goals):
            source = goal_ref.at[0] if group == 0 else premise_ref.at[
                0, pl.ds((group - 1) * goals, goals)
            ]
            pltpu.make_async_copy(
                source, arrived.at[pl.ds(group * goals, goals)], semaphores.at[group]
            ).start()
        end = (last + 1) * CHUNK
        edge = jnp.zeros((EDGE, width), BF16)
        padded_low[:EDGE, :] = edge
        padded_up[:EDGE, :] = edge
        padded_up[pl.ds(pl.multiple_of(EDGE + end, EDGE), EDGE), :] = edge
        padded_low[pl.ds(pl.multiple_of(EDGE + end, EDGE), EDGE), :] = edge
        mix_gain[...] = (depth_ref[...] * gain_ref[...]).astype(BF16)
        summary_ref[...] = jnp.zeros_like(summary_ref)
        pooling[0] = table_of(scalars, 0, count, (count, 1), 0)
        pooling[1] = table_of(scalars, count, count, (count, 1), 0)
        next_sequence[0] = 0

    @pl.when(step <= last)
    def _():
        def clear(at):
            at = pl.multiple_of(at, TILE)
            states[pl.ds(at, TILE), :] = jnp.zeros((TILE, width), BF16)
            valid_rows[pl.ds(at, TILE), :] = jnp.zeros((TILE, LANES), F32)

        def wanted(seq):
            inside = jnp.minimum(seq, count - 1)
            return (seq < count) & (scalars[count + inside] < (step + 1) * CHUNK)

        def one_sequence(seq):
            @pl.when(lax.rem(seq, goals) == 0)
            def _():
                pltpu.make_async_copy(
                    goal_ref.at[0],
                    arrived.at[pl.ds(seq, goals)],
                    semaphores.at[lax.div(seq, goals)],
                ).wait()

            used, offset = scalars[seq], scalars[count + seq]

            def part(index, carry):
                start = pl.multiple_of(index * PART, PART)
                at = pl.ds(pl.multiple_of(offset + start, TILE), PART)
                states[at, :] = arrived[seq, pl.ds(start, PART), :]
                valid_rows[at, :] = jnp.where(row_of < used - start, 1.0, 0.0)
                return carry

            parts = (used + PART - 1) // PART
            lax.fori_loop(0, parts, part, 0)
            clear(offset + parts * PART)
            return seq + 1

        next_sequence[0] = lax.while_loop(wanted, one_sequence, next_sequence[0])

        @pl.when(step == last)
        def _():
            def clear_tail(tile, carry):
                clear(scalars[2 * count] + tile * TILE)
                return carry

            spare = (last + 1) * CHUNK - scalars[2 * count]
            lax.fori_loop(0, lax.div(spare, TILE), clear_tail, 0)

    def staged(first, second):
        for block in range(0, CHUNK + SUB, SUB):
            if block < CHUNK:
                first(block)
            if block:
                second(block - SUB)

    def rows_of(block):
        return range(block, block + SUB, TILE)

    def window_of(padded, base, start):
        return padded[pl.ds(pl.multiple_of(base + start, TILE), TILE + 2 * EDGE), :]

    def inverse_of(base, block):
        mean = jnp.dot(
            squares[block : block + SUB, :], ones, preferred_element_type=F32
        ) * (1.0 / width)
        place = pl.ds(pl.multiple_of(base + block, TILE), SUB)
        return (lax.rsqrt(mean + EPS) * valid_rows[place, :]).astype(BF16)

    @pl.when(step <= last)
    def _():
        base = step * CHUNK

        def square(block):
            raw = states[pl.ds(pl.multiple_of(base + block, TILE), SUB), :]
            squares[block : block + SUB, :] = raw * raw

        def scale(block):
            inverse = wide(inverse_of(base, block))
            raw = states[pl.ds(pl.multiple_of(base + block, TILE), SUB), :]
            padded_low[pl.ds(pl.multiple_of(EDGE + base + block, EDGE), SUB), :] = raw * inverse

        staged(square, scale)

    @pl.when((step >= 1) & (step <= last + 1))
    def _():
        base = (step - 1) * CHUNK
        slot = lax.rem(step + 1, 2)

        def mix_low(block):
            for start in rows_of(block):
                window = window_of(padded_low, base, start)
                at = pl.ds(start, TILE)
                total = None
                for tap in range(3):
                    first = EDGE + (tap - 1) * LOWER_DILATION
                    values = window[first : first + TILE]
                    term = mix_gain[tap, 0:1, :] * values
                    total = term if total is None else total + term
                    if tap == 1:
                        normed_low_ref[at, :] = values
                mixed[at, :] = total
            at = pl.ds(block, SUB)
            pre_act[at, :] = jnp.dot(
                mixed[at, :], weight_ref[0], preferred_element_type=F32
            ).astype(BF16)

        def act_low(block):
            for start in rows_of(block):
                at = pl.ds(start, TILE)
                place = pl.ds(pl.multiple_of(base + start, TILE), TILE)
                value, slope = gelu_parts(pre_act[at, :])
                slope_low_ref[at, :] = slope
                out = states[place, :] + value
                hidden[slot, at, :] = out
                squares[at, :] = out * out
            at = pl.ds(block, SUB)
            inverse = inverse_of(base, block)
            inverse_ref[at, :] = inverse
            normed = hidden[slot, at, :] * wide(inverse)
            padded_up[pl.ds(pl.multiple_of(EDGE + base + block, EDGE), SUB), :] = normed
            normed_up_ref[at, :] = normed

        staged(mix_low, act_low)

    @pl.when((step >= 2) & (step <= last + 2))
    def _():
        base = (step - 2) * CHUNK
        slot = lax.rem(step, 2)

        def mix_up(block):
            for start in rows_of(block):
                window = window_of(padded_up, base, start)
                total = None
                for tap in range(3):
                    first = EDGE + (tap - 1) * UPPER_DILATION
                    term = mix_gain[tap, 1:2, :] * window[first : first + TILE]
                    total = term if total is None else total + term
                mixed_up_ref[pl.ds(start, TILE), :] = total
            at = pl.ds(block, SUB)
            pre_act[at, :] = jnp.dot(
                mixed_up_ref[at, :], weight_ref[1], preferred_element_type=F32
            ).astype(BF16)

        def act_up(block):
            for start in rows_of(block):
                at = pl.ds(start, TILE)
                value, slope = gelu_parts(pre_act[at, :])
                slope_up_ref[at, :] = slope
                mixed[at, :] = hidden[slot, at, :] + value

        staged(mix_up, act_up)
        place = base + lax.broadcasted_iota(jnp.int32, (count, CHUNK), 1)
        begin = pooling[1]
        member = (place >= begin) & (place < begin + pooling[0])
        summary_ref[:, :width] += jnp.dot(
            jnp.where(member, 1.0, 0.0).astype(BF16), mixed[...], preferred_element_type=F32
        )

    @pl.when(step == pl.num_programs(0) - 1)
    def _():
        pooled = summary_ref[:, :width] / pooling[0].astype(F32)
        summary_ref[:, :width] = pooled
        embedded = jnp.dot(pooled.astype(BF16), head_ref[...], preferred_element_type=F32)
        magnitude = jnp.sqrt(jnp.sum(embedded * embedded, axis=-1, keepdims=True) + EPS)
        unit = embedded / magnitude
        embed = unit.shape[1]
        summary_ref[:, width : width + embed] = unit
        summary_ref[:, width + embed :] = jnp.broadcast_to(magnitude, (count, LANES))
        rounded = unit.astype(BF16)
        for peer in range(N_NEG):
            spread_ref[peer] = rounded


def backward_kernel(
    scalars,
    gathered_ref,
    summary_ref,
    column_target_ref,
    head_ref,
    depth_ref,
    gain_ref,
    weight_ref,
    normed_low_ref,
    slope_low_ref,
    normed_up_ref,
    inverse_ref,
    mixed_up_ref,
    slope_up_ref,
    loss_ref,
    keep_ref,
    send_ref,
    pooled_grad,
    members,
    upstream,
    grad_up,
    grad_low,
    conv_grad,
    normed_low,
    shifted,
    mixed_low,
    scaled,
    products,
    squares,
    corr,
    point_up,
    point_low,
    head_grad,
    mix_half,
    semaphore,
):
    step = pl.program_id(0)
    last = pl.num_programs(0) - 1
    count = summary_ref.shape[0]
    position, core = scalars[2 * count + 1], scalars[2 * count + 2]
    width = grad_up.shape[1]
    rows = normed_low_ref.shape[0]
    final = last_chunk(scalars, count)

    after = pl.multiple_of(EDGE + (final + 1) * CHUNK, EDGE)

    def load_normed():
        return pltpu.make_async_copy(
            normed_low_ref, normed_low.at[pl.ds(EDGE, rows)], semaphore.at[0]
        )

    @pl.when(step == 0)
    def _():
        load_normed().start()
        zeros = jnp.zeros((EDGE, width), BF16)
        conv_grad[:EDGE, :] = zeros
        conv_grad[pl.ds(after, EDGE), :] = zeros
        mix_half[...] = (depth_ref[...] * gain_ref[...]).astype(BF16)
        members[0] = table_of(scalars, 0, count, (8, count), 1)
        members[1] = table_of(scalars, count, count, (8, count), 1)
        corr[...] = jnp.zeros_like(corr)
        point_up[...] = jnp.zeros_like(point_up)
        point_low[...] = jnp.zeros_like(point_low)
        every = gathered_ref[...]
        total_count = every.shape[0]
        own_count = count
        embed = every.shape[1]
        unit = summary_ref[:, width : width + embed]
        magnitude = summary_ref[:, width + embed : width + embed + 1]
        contract = (((1,), (1,)), ((), ()))
        gram = lax.dot_general(every, every, contract, preferred_element_type=F32)
        row_of = lax.broadcasted_iota(jnp.int32, (total_count, 1), 0)
        row_goal = lax.rem(row_of, own_count) < goal_total
        expon = jnp.where(row_goal, 0.0, jnp.exp(logit_scale * gram))
        column_total = jnp.sum(expon, axis=0, keepdims=True)
        scores = logit_scale * lax.dot_general(
            unit.astype(BF16), every, contract, preferred_element_type=F32
        )
        own_expon = jnp.exp(scores)
        column_of = lax.broadcasted_iota(jnp.int32, (own_count, total_count), 1)
        column_goal = lax.rem(column_of, own_count) < goal_total
        own_goal = lax.broadcasted_iota(jnp.int32, (own_count, total_count), 0) < goal_total
        own_total = jnp.sum(
            jnp.where(column_goal, 0.0, own_expon), axis=1, keepdims=True
        )
        own_index = position * own_count + lax.broadcasted_iota(
            jnp.int32, (own_count, total_count), 0
        )
        targets = column_target_ref[...]
        own_target = jnp.sum(
            jnp.where(column_of == own_index, targets.astype(F32), 0.0), axis=1, keepdims=True
        ).astype(jnp.int32)
        hit_goal = column_of == own_target
        hit_premise = targets == own_index
        of_goal = own_expon / own_total - jnp.where(hit_goal, 1.0, 0.0)
        of_premise = own_expon / column_total - jnp.where(hit_premise, 1.0, 0.0)
        score_grad = jnp.where(
            own_goal,
            jnp.where(column_goal, 0.0, of_goal),
            jnp.where(column_goal, of_premise, 0.0),
        )
        score_grad = (score_grad / float(goal_total)).astype(BF16)
        chosen = jnp.sum(jnp.where(hit_goal, scores, 0.0), axis=1, keepdims=True)
        loss_ref[...] = jnp.broadcast_to(jnp.log(own_total) - chosen, loss_ref.shape)
        unit_grad = logit_scale * jnp.dot(score_grad, every, preferred_element_type=F32)
        along = jnp.sum(unit * unit_grad, axis=-1, keepdims=True)
        embed_grad = ((unit_grad - unit * along) / magnitude).astype(BF16)
        head_grad[...] = lax.dot_general(
            summary_ref[:, :width].astype(BF16),
            embed_grad,
            (((0,), (0,)), ((), ())),
            preferred_element_type=F32,
        ).astype(BF16)
        used = table_of(scalars, 0, count, (count, 1), 0)
        spread_back = lax.dot_general(
            embed_grad, head_ref[...], contract, preferred_element_type=F32
        ) / used.astype(F32)
        pooled_grad[...] = spread_back.astype(BF16)

    over_tokens = (((0,), (0,)), ((), ()))
    turned = (((1,), (1,)), ((), ()))
    blocks = range(0, CHUNK, SUB)

    @pl.when(step == 1)
    def _():
        load_normed().wait()
        zeros = jnp.zeros((EDGE, width), BF16)
        normed_low[:EDGE, :] = zeros
        normed_low[pl.ds(after, EDGE), :] = zeros

    @pl.when(step <= final)
    def _():
        base = step * CHUNK
        slot = lax.rem(step, 2)
        begin = members[1, 0:1, :]
        end = begin + members[0, 0:1, :]
        for block in blocks:
            at = pl.ds(block, SUB)
            place = base + block + lax.broadcasted_iota(jnp.int32, (SUB, count), 0)
            member = jnp.where((place >= begin) & (place < end), 1.0, 0.0).astype(BF16)
            above = jnp.dot(member, pooled_grad[...], preferred_element_type=F32).astype(BF16)
            upstream[slot, at, :] = above
            grad = slope_up_ref[at, :] * above
            grad_up[at, :] = grad
            conv_grad[pl.ds(pl.multiple_of(EDGE + base + block, EDGE), SUB), :] = (
                lax.dot_general(
                    grad, weight_ref[1], turned, preferred_element_type=F32
                ).astype(BF16)
            )
        point_up[...] += lax.dot_general(
            mixed_up_ref[...], grad_up[...], over_tokens, preferred_element_type=F32
        )

    @pl.when((step >= 1) & (step <= final + 1))
    def _():
        base = (step - 1) * CHUNK
        slot = lax.rem(step + 1, 2)
        ones = jnp.ones((width, LANES), BF16)

        def window_of(array, start):
            place = pl.ds(pl.multiple_of(base + start, TILE), TILE + 2 * EDGE)
            return array[place, :]

        def gather(sums, first, start, tap, product):
            sums[tap] = product if start % GROUP == 0 else sums[tap] + product
            if (start + TILE) % GROUP == 0:
                kept = start // GROUP * TILE
                products[first + tap, kept : kept + TILE, :] = sums[tap]

        def mix(block):
            sums = [None] * 3
            for start in range(block, block + SUB, TILE):
                at = pl.ds(start, TILE)
                window = window_of(conv_grad, start)
                states = window_of(normed_low, start)
                normed = normed_up_ref[at, :]
                total = low = None
                for tap in range(3):
                    first = EDGE + (1 - tap) * UPPER_DILATION
                    part = window[first : first + TILE]
                    term = mix_half[tap, 1:2, :] * part
                    total = term if total is None else total + term
                    gather(sums, 3, start, tap, part * normed)
                    first = EDGE + (tap - 1) * LOWER_DILATION
                    values = states[first : first + TILE]
                    shifted[tap, at, :] = values
                    term = mix_half[tap, 0:1, :] * values
                    low = term if low is None else low + term
                mixed_low[at, :] = low
                scaled[at, :] = total
                squares[at, :] = total * normed

        def back(block):
            at = pl.ds(block, SUB)
            mean = (
                jnp.dot(squares[at, :], ones, preferred_element_type=F32) * (1.0 / width)
            ).astype(BF16)
            inner = scaled[at, :] - normed_up_ref[at, :] * wide(mean)
            below = upstream[slot, at, :] + wide(inverse_ref[at, :]) * inner
            grad = below * slope_low_ref[at, :]
            grad_low[at, :] = grad
            scaled[at, :] = lax.dot_general(
                grad, weight_ref[0], turned, preferred_element_type=F32
            ).astype(BF16)

        def correlate(block):
            sums = [None] * 3
            for start in range(block, block + SUB, TILE):
                conv = scaled[start : start + TILE, :]
                for tap in range(3):
                    gather(sums, 0, start, tap, conv * shifted[tap, start : start + TILE, :])

        for block in range(0, CHUNK + 2 * SUB, SUB):
            if block < CHUNK:
                mix(block)
            if 0 <= block - SUB < CHUNK:
                back(block - SUB)
            if block >= 2 * SUB:
                correlate(block - 2 * SUB)
        every_row = jnp.ones((8, CHUNK // GROUP * TILE), BF16)
        for index in range(6):
            corr[index] += jnp.dot(every_row, products[index], preferred_element_type=F32)
        point_low[...] += lax.dot_general(
            mixed_low[...], grad_low[...], over_tokens, preferred_element_type=F32
        )

    def emit(low_ref, up_ref):
        rows = [corr[index, 0:1, :] for index in range(6)]
        rows.append(jnp.zeros((2, width), F32))
        small = jnp.concatenate(rows, axis=0)
        low = point_low[...].astype(BF16)
        up = point_up[...].astype(BF16)
        for part in range(width // LANES):
            lanes = slice(part * LANES, (part + 1) * LANES)
            low_ref[part * width : (part + 1) * width, :] = low[:, lanes]
            up_ref[part * width : (part + 1) * width, :] = up[:, lanes]
        base = width * width // LANES
        for part in range(head_grad.shape[1] // LANES):
            lanes = slice(part * LANES, (part + 1) * LANES)
            low_ref[base + part * width : base + (part + 1) * width, :] = head_grad[:, lanes]
        tail = [small[:, part * LANES : (part + 1) * LANES] for part in range(width // LANES)]
        up_ref[base : base + 32, :] = jnp.concatenate(tail, axis=0).astype(BF16)
        up_ref[base + 32 :, :] = jnp.zeros((up_ref.shape[0] - base - 32, LANES), BF16)

    @pl.when((step == last) & (core == 0))
    def _():
        emit(keep_ref, send_ref)

    @pl.when((step == last) & (core == 1))
    def _():
        emit(send_ref, keep_ref)


def unpack_kernel(
    scalars,
    mine_ref,
    other_ref,
    depth_ref,
    gain_ref,
    depth_out,
    gain_out,
    point_out,
    head_out,
):
    core = scalars[scalars.shape[0] - 1]
    width = gain_ref.shape[1]
    base = width * width // LANES

    def emit(low_ref, up_ref):
        for part in range(width // LANES):
            lanes = slice(part * LANES, (part + 1) * LANES)
            rows = slice(part * width, (part + 1) * width)
            point_out[0, :, lanes] = low_ref[rows, :].astype(F32)
            point_out[1, :, lanes] = up_ref[rows, :].astype(F32)
        for part in range(head_out.shape[1] // LANES):
            lanes = slice(part * LANES, (part + 1) * LANES)
            head_out[:, lanes] = low_ref[
                base + part * width : base + (part + 1) * width, :
            ].astype(F32)
        small = up_ref[base : base + 32, :].astype(F32)
        for part in range(width // LANES):
            lanes = slice(part * LANES, (part + 1) * LANES)
            rows = small[part * 8 : (part + 1) * 8, :]
            for block in range(2):
                total = 0.0
                for tap in range(3):
                    row = rows[block * 3 + tap : block * 3 + tap + 1, :]
                    depth_out[tap, block : block + 1, lanes] = (
                        row * gain_ref[block : block + 1, lanes]
                    )
                    total = total + row * depth_ref[tap, block : block + 1, lanes]
                gain_out[block : block + 1, lanes] = total

    @pl.when(core == 0)
    def _():
        emit(mine_ref, other_ref)

    @pl.when(core == 1)
    def _():
        emit(other_ref, mine_ref)


goal_total = 8


def whole(shape):
    return pl.BlockSpec(shape, lambda i, *_: (0,) * len(shape))


def run_forward(scalars, goal_states, premise_states, depth, gains, weights, head_weight):
    goals, length, width = goal_states.shape[1:]
    premises = premise_states.shape[1]
    count = goals + premises
    embed = head_weight.shape[1]
    chunks = -(-count * (length + TILE) // CHUNK)
    rows = chunks * CHUNK
    summary = (count, width + embed + LANES)

    def lower(columns):
        return pl.BlockSpec(
            (CHUNK, columns), lambda i, s: (jnp.clip(i - 1, 0, last_chunk(s, count)), 0)
        )

    upper = pl.BlockSpec(
        (CHUNK, width), lambda i, s: (jnp.clip(i - 2, 0, last_chunk(s, count)), 0)
    )
    packed = jax.ShapeDtypeStruct((rows, width), BF16)
    outs = [
        (packed, lower(width)),
        (packed, lower(width)),
        (packed, lower(width)),
        (jax.ShapeDtypeStruct((rows, LANES), BF16), lower(LANES)),
        (packed, upper),
        (packed, upper),
        (jax.ShapeDtypeStruct(summary, F32), whole(summary)),
        (
            jax.ShapeDtypeStruct((N_NEG, count, embed), BF16),
            whole((N_NEG, count, embed)),
        ),
    ]
    raw = pl.BlockSpec(memory_space=pl.ANY)
    return pl.pallas_call(
        forward_kernel,
        name="forward",
        out_shape=[o[0] for o in outs],
        grid_spec=pltpu.PrefetchScalarGridSpec(
            num_scalar_prefetch=1,
            grid=(chunks + 2,),
            in_specs=[
                raw,
                raw,
                whole(depth.shape),
                whole(gains.shape),
                whole(weights.shape),
                whole(head_weight.shape),
            ],
            out_specs=[o[1] for o in outs],
            scratch_shapes=[
                pltpu.VMEM((count, length, width), BF16),
                pltpu.VMEM((rows + PART + TILE, width), BF16),
                pltpu.VMEM((rows + PART + TILE, LANES), F32),
                pltpu.VMEM((rows + 2 * EDGE, width), BF16),
                pltpu.VMEM((rows + 2 * EDGE, width), BF16),
                pltpu.VMEM((2, CHUNK, width), BF16),
                pltpu.VMEM((CHUNK, width), BF16),
                pltpu.VMEM((CHUNK, width), BF16),
                pltpu.VMEM((CHUNK, width), BF16),
                pltpu.VMEM((2, count, 1), jnp.int32),
                pltpu.VMEM(depth.shape, BF16),
                pltpu.SemaphoreType.DMA((count // goals,)),
                pltpu.SMEM((1,), jnp.int32),
            ],
        ),
        compiler_params=pltpu.CompilerParams(
            dimension_semantics=("arbitrary",), vmem_limit_bytes=60 << 20
        ),
    )(scalars, goal_states, premise_states, depth, gains, weights, head_weight)


def run_backward(scalars, tables, residuals):
    rows, width = residuals[1].shape
    count = tables[1].shape[0]
    embed = tables[0].shape[1]
    depth = tables[4]
    half = (N_NEG * N_REP // 2 * SLICE, LANES)
    outs = [
        jax.ShapeDtypeStruct((count, LANES), F32),
        jax.ShapeDtypeStruct(half, BF16),
        jax.ShapeDtypeStruct(half, BF16),
    ]
    specs = [whole(t.shape) for t in tables]

    def early(array):
        return pl.BlockSpec(
            (CHUNK, array.shape[1]), lambda i, s: (jnp.minimum(i, last_chunk(s, count)), 0)
        )

    def late(array):
        return pl.BlockSpec(
            (CHUNK, array.shape[1]),
            lambda i, s: (jnp.clip(i - 1, 0, last_chunk(s, count)), 0),
        )

    return pl.pallas_call(
        backward_kernel,
        name="backward",
        out_shape=outs,
        grid_spec=pltpu.PrefetchScalarGridSpec(
            num_scalar_prefetch=1,
            grid=(rows // CHUNK + 1,),
            in_specs=specs
            + [pl.BlockSpec(memory_space=pl.ANY)]
            + [late(r) for r in residuals[1:4]]
            + [early(r) for r in residuals[4:]],
            out_specs=[whole(o.shape) for o in outs],
            scratch_shapes=[
                pltpu.VMEM((count, width), BF16),
                pltpu.VMEM((2, 8, count), jnp.int32),
                pltpu.VMEM((2, CHUNK, width), BF16),
                pltpu.VMEM((CHUNK, width), BF16),
                pltpu.VMEM((CHUNK, width), BF16),
                pltpu.VMEM((rows + 2 * EDGE, width), BF16),
                pltpu.VMEM((rows + 2 * EDGE, width), BF16),
                pltpu.VMEM((3, CHUNK, width), BF16),
                pltpu.VMEM((CHUNK, width), BF16),
                pltpu.VMEM((CHUNK, width), BF16),
                pltpu.VMEM((6, CHUNK // GROUP * TILE, width), BF16),
                pltpu.VMEM((CHUNK, width), BF16),
                pltpu.VMEM((6, 8, width), F32),
                pltpu.VMEM((width, width), F32),
                pltpu.VMEM((width, width), F32),
                pltpu.VMEM((width, embed), BF16),
                pltpu.VMEM(depth.shape, BF16),
                pltpu.SemaphoreType.DMA((1,)),
            ],
        ),
        compiler_params=pltpu.CompilerParams(
            dimension_semantics=("arbitrary",), vmem_limit_bytes=60 << 20
        ),
    )(scalars, *tables, *residuals)


def reduce_everywhere(scalars, keep, send, depth, gains, embed):
    peers = N_NEG * N_REP // 2
    axes = ("neg", "chip")
    swap = [(0, 1), (1, 0)]
    width = gains.shape[1]
    got = lax.ppermute(send, "core", swap)
    pair = (keep.astype(F32) + got.astype(F32)).astype(BF16)
    parts = lax.all_to_all(pair.reshape(peers, SLICE, LANES), axes, 0, 0)
    total = jnp.sum(parts.astype(F32), axis=0).astype(BF16)
    spread = jnp.broadcast_to(total[None], parts.shape)
    mine = lax.all_to_all(spread, axes, 0, 0).reshape(peers * SLICE, LANES)
    other = lax.ppermute(mine, "core", swap)
    vmem = pl.BlockSpec(memory_space=pltpu.VMEM)
    return pl.pallas_call(
        unpack_kernel,
        name="unpack",
        in_specs=[pl.BlockSpec(memory_space=pltpu.SMEM)] + [vmem] * 4,
        out_specs=[vmem] * 4,
        out_shape=[
            jax.ShapeDtypeStruct(depth.shape, F32),
            jax.ShapeDtypeStruct(gains.shape, F32),
            jax.ShapeDtypeStruct((2, width, width), F32),
            jax.ShapeDtypeStruct((width, embed), F32),
        ],
    )(scalars, mine, other, depth, gains)


def local(
    goal_states,
    premise_states,
    goal_ids,
    premise_ids,
    positives,
    depthwise_kernels,
    block_norm_gains,
    pointwise_weights,
    head_weight,
):
    goals = goal_states.shape[1]
    premises = premise_states.shape[1]
    count = goals + premises
    position = lax.axis_index("neg")
    lengths = jnp.sum(
        (jnp.concatenate([goal_ids[0], premise_ids[0]], axis=0) != 0).astype(jnp.int32), axis=1
    )
    room = (lengths + (PAD + TILE - 1)) // TILE * TILE
    places = jnp.arange(count + 1)
    starts = jnp.sum(
        jnp.where(places[None, :count] < places[:, None], room[None, :], 0), axis=1
    )
    scalars = jnp.concatenate(
        [lengths, starts, jnp.stack([position, lax.axis_index("core")])]
    ).astype(jnp.int32)
    depth = depthwise_kernels.transpose(1, 0, 2)
    outs = run_forward(
        scalars,
        goal_states,
        premise_states,
        depth,
        block_norm_gains,
        pointwise_weights,
        head_weight,
    )
    residuals, (summary, spread) = outs[:6], outs[6:]
    gathered = lax.all_to_all(spread, "neg", 0, 0).reshape(N_NEG * count, -1)
    slot = positives[0] // premises * count + goals + positives[0] % premises
    slot = jnp.concatenate(
        [
            slot.reshape(N_NEG, goals).astype(jnp.int32),
            jnp.full((N_NEG, premises), -1, jnp.int32),
        ],
        axis=1,
    )
    tables = (
        gathered,
        summary,
        slot.reshape(1, N_NEG * count),
        head_weight,
        depth,
        block_norm_gains,
        pointwise_weights,
    )
    loss, keep, send = run_backward(scalars, tables, residuals)
    depth_grad, gain_grad, point_grad, head_grad = reduce_everywhere(
        scalars, keep, send, depth, block_norm_gains, head_weight.shape[1]
    )
    return (
        loss[:goals, 0][None, :],
        depth_grad.transpose(1, 0, 2),
        gain_grad,
        point_grad,
        head_grad,
    )


def solution(mesh):
    split = Mesh(mesh.devices.reshape(N_NEG, N_REP // 2, 2), ("neg", "chip", "core"))
    group = ("chip", "core")
    placed = (
        P(group, "neg", None, None),
        P(group, "neg", None, None),
        P(group, "neg", None),
        P(group, "neg", None),
        P(group, None),
        P(),
        P(),
        P(),
        P(),
    )
    return jax.shard_map(
        local,
        mesh=split,
        in_specs=placed,
        out_specs=(P(group, "neg"), P(), P(), P(), P()),
        check_vma=False,
    )
```
